32 devices in a mesh: axial: 16 (over z, x, core), azim: 2 (over y).
Axes of the slice: x: 2, y: 2, z: 4, core: 2. Of those that a mesh axis runs over, the one named last changes fastest.
Arguments:
- adjoint_source: float32 [32, 4, 5, 15, 128], P('axial', 'azim'), may hold values from -0.6 to 0.6
- adjoint_prev: float32 [32, 4, 5, 15, 128], P('axial', 'azim'), may hold values from -1.8 to 1.8
- diag_inverse: bfloat16 [32, 4, 5, 5, 15, 128], P('axial', 'azim'), may hold values from -0.1 to 1
- coupling: float32 [3, 32, 4, 15, 128], P(None, 'axial', 'azim'), may hold values from 0.1 to 1.03
- spectral: float32 [15, 15], replicated, may hold values from -0.6 to 0.6
- face_map: int32 [512], P('azim'), may hold values from 0 to 511, each once
Outputs:
- adjoint: float32 [32, 4, 5, 15, 128], P('axial', 'azim')
The draws below stay inside these ranges and needn't reach their ends.
Inputs may be any that keep to these rules, and one draw needn't show every extreme that they name: `face_map`: each rudder interface cell is named by exactly one propeller interface cell.
All inputs are finite; a program needn't handle non-finite values.
Results may differ from the reference program's by a relative error of at most 0.0003.
Values sent between devices are 32-bit elements; how exact they have to be, the bound alone decides.
No kernel may reach another device: no remote copies, remote signals or barrier semaphores. Data moves between devices by JAX's collectives and lax.ppermute only.
A program may use at most 64 MiB of HBM per device.

```python
import math
import jax
import jax.numpy as jnp
from jax import lax

F = 5
TIME_INSTANCES = 15
ITERS = 2
CA = 2
NR = 128
AXIAL_PLANES = 32
NP = 4


def draw_diag_inverse(key, part):
    child_keys = jax.random.split(key, 2)
    lowest = 0.92
    diagonal = jax.random.uniform(child_keys[0], (AXIAL_PLANES, NP, F, 1, TIME_INSTANCES, NR), jnp.float32, lowest, 1.0)
    offdiag = jax.random.uniform(child_keys[1], (AXIAL_PLANES, NP, F, F, TIME_INSTANCES, NR), jnp.float32, -0.0995, 0.0995)
    unit = jnp.eye(F, dtype=jnp.float32)[None, None, :, :, None, None]
    return (unit * diagonal + (1.0 - unit) * offdiag).astype(jnp.bfloat16)


def draw_coupling(key, part):
    child_keys = jax.random.split(key, 8)
    chan_shape = (2, 1, NP, TIME_INSTANCES, NR)
    share = 0.5
    chosen = jax.random.uniform(child_keys[0], chan_shape, jnp.float32) < share
    slow_rate = jnp.exp(jax.random.uniform(child_keys[1], chan_shape, jnp.float32, math.log(0.004), math.log(0.015)))
    fast_rate = jnp.exp(jax.random.uniform(child_keys[2], chan_shape, jnp.float32, math.log(0.07), math.log(0.12)))
    channel_rate = jnp.where(chosen, slow_rate, fast_rate)
    processor_factor = jnp.exp(jax.random.uniform(child_keys[3], (2, AXIAL_PLANES // CA, 1, TIME_INSTANCES, 1), jnp.float32, math.log(0.5), math.log(2.0)))
    processor_factor = jnp.repeat(processor_factor, CA, axis=1)
    coarse_estimate = jax.random.uniform(child_keys[4], (2, AXIAL_PLANES, NP, TIME_INSTANCES, NR), jnp.float32, 0.6, 1.6)
    surge_triggered = jax.random.uniform(child_keys[5], (2, AXIAL_PLANES, 1, TIME_INSTANCES, 1), jnp.float32) < 3.0 / AXIAL_PLANES
    surge_retained = jax.random.uniform(child_keys[6], (2, AXIAL_PLANES, 1, TIME_INSTANCES, 1), jnp.float32, 0.5, 0.8)
    linked_sequence = (1.0 - channel_rate * processor_factor * coarse_estimate) * 1.03 * jnp.where(surge_triggered, surge_retained, 1.0)
    side_coef = jax.random.uniform(child_keys[7], (1, AXIAL_PLANES, NP, TIME_INSTANCES, NR), jnp.float32, 0.1, 0.3)
    return jnp.concatenate([linked_sequence, side_coef], axis=0)


def shard_levels(stream_key, shape, cuts, least, top_value):
    loudness, own = 1.0, jax.random.fold_in(stream_key, 6)
    for axis_at, parts in cuts:
        heights = jnp.exp(jax.random.uniform(jax.random.fold_in(own, axis_at), (parts,), jnp.float32, least / len(cuts), top_value / len(cuts)))
        loudness = loudness * jnp.repeat(heights, shape[axis_at] // parts).reshape([-1 if axis == axis_at else 1 for axis in range(len(shape))])
    return loudness


def scatter_about(stream_key, dims, spread, reach, cuts=(), kind=jnp.bfloat16):
    values = spread * jax.random.normal(stream_key, dims, jnp.float32)
    if cuts:
        values = values * shard_levels(stream_key, dims, cuts, -0.22, 0.18)
    return jnp.clip(values, -reach, reach).astype(kind)


def setup_inputs(seed: int = 0) -> dict:
    streams_of = jax.random.split(jax.random.key(seed), 7)
    return {
        "adjoint_source": scatter_about(streams_of[0], (AXIAL_PLANES, NP, F, TIME_INSTANCES, NR), 0.1, 0.6, ((0, 16), (1, 2)), jnp.float32),
        "adjoint_prev": scatter_about(streams_of[1], (AXIAL_PLANES, NP, F, TIME_INSTANCES, NR), 0.3, 1.8, ((0, 16), (1, 2)), jnp.float32),
        "diag_inverse": draw_diag_inverse(jax.random.fold_in(streams_of[6], 71), 0),
        "coupling": draw_coupling(jax.random.fold_in(streams_of[6], 71), 0),
        "spectral": scatter_about(streams_of[4], (TIME_INSTANCES, TIME_INSTANCES), 0.1, 0.6, (), jnp.float32),
        "face_map": jax.random.permutation(streams_of[5], NP * NR).astype(jnp.int32),
    }


def apply_inverse(inverse, vector):
    return jnp.sum(inverse.astype(jnp.float32) * vector[:, None], axis=2)


def make_rhs(source, lower_rim, upper_rim, previous, side_coef, spectral):
    coupled = jnp.einsum('hk,...kr->...hr', spectral, previous, precision=lax.Precision.HIGHEST)
    return source + jnp.expand_dims(side_coef, -3) * (lower_rim + upper_rim) - coupled


def forward_section(right_side, inverse, lower_coef):
    def plane_step(carried, plane_items):
        plane_source, plane_inverse, plane_coef = plane_items
        fresh = apply_inverse(plane_inverse, plane_source + jnp.expand_dims(plane_coef, -3) * carried)
        return fresh, fresh
    start_vals = jnp.zeros(right_side.shape[1:], jnp.float32)
    unused, values = lax.scan(plane_step, start_vals, (right_side, inverse, lower_coef))
    return values


def backward_section(front_vals, inverse, upper_coef, boundary):
    def plane_step(carried, plane_items):
        plane_front, plane_inverse, plane_coef = plane_items
        fresh = plane_front - jnp.expand_dims(plane_coef, -3) * apply_inverse(plane_inverse, carried)
        return fresh, fresh
    unused, values = lax.scan(plane_step, boundary, (front_vals, inverse, upper_coef), reverse=True)
    return values


def reference(adjoint_source, adjoint_prev, diag_inverse, coupling, spectral, face_map):
    section = AXIAL_PLANES // 2
    current = adjoint_prev
    lower_coef, upper_coef, side_coef = coupling[0], coupling[1], coupling[2]
    for sweep_index in range(ITERS):
        right_side = make_rhs(adjoint_source, jnp.roll(current, 1, axis=1), jnp.roll(current, -1, axis=1), current, side_coef, spectral)
        plane_flat = jnp.transpose(current[section], (1, 2, 0, 3)).reshape(F * TIME_INSTANCES, NP * NR)
        picked = jnp.take(plane_flat, face_map, axis=1).reshape(F, TIME_INSTANCES, NP, NR).transpose(2, 0, 1, 3)
        pieces = []
        for first_plane, boundary in ((0, picked), (section, jnp.zeros_like(picked))):
            front_vals = forward_section(right_side[first_plane:first_plane + section], diag_inverse[first_plane:first_plane + section], lower_coef[first_plane:first_plane + section])
            pieces.append(backward_section(front_vals, diag_inverse[first_plane:first_plane + section], upper_coef[first_plane:first_plane + section], boundary))
        current = jnp.concatenate(pieces, axis=0)
    return current
```

```python
import functools

import jax
import jax.numpy as jnp
from jax import lax
from jax.experimental import pallas as pl
from jax.experimental.pallas import tpu as pltpu
from jax.sharding import PartitionSpec as P

F = 5
HP = 16
LANES = 128
LOWER, UPPER, SIDE, SOURCE, RIGHT, ITEMS = 25, 26, 27, 28, 33, 38
HIGHEST = lax.Precision.HIGHEST


def params():
    return pltpu.CompilerParams(vmem_limit_bytes=48 * 2**20)


def matvec(matrix, vector):
    out = []
    for f in range(F):
        terms = [matrix(f * F + g) * vector[g] for g in range(F)]
        out.append((terms[0] + terms[1]) + (terms[2] + terms[3]) + terms[4])
    return out


def pack_kernel(
    n, azim, source, prev, left, right, diag, coupling, spectral, face, *rest
):
    facing, (out, cells, turned, mix, prod) = rest[:azim], rest[azim:]
    planes, rows, _, inst, _ = source.shape
    mine = lax.axis_index("azim")
    part = LANES // n
    per_row = LANES // part
    halves = HP // per_row
    count = rows * planes * ITEMS
    cells[:, HP - 1, :] = jnp.zeros((count, LANES), jnp.float32)
    mix[...] = jnp.zeros_like(mix)
    mix[0:inst, 0:inst] = spectral[...]
    prod[HP - 1 :, :] = jnp.zeros((1, prod.shape[1]), jnp.float32)
    for a in range(planes):
        for j in range(rows):
            for f in range(F):
                at = ((a * rows + j) * F + f) * LANES
                prod[0:inst, at : at + LANES] = prev[a, j, f]
    prod[...] = jnp.dot(mix[...], prod[...], precision=HIGHEST, preferred_element_type=jnp.float32)
    picked = []
    for j in range(rows):
        cell = jnp.broadcast_to(face[j : j + 1, :], (inst, LANES))
        accs = [jnp.zeros((inst, LANES), jnp.float32)] * F
        for k in range(azim):
            origin = lax.rem(mine - k + azim, azim) * rows
            for p in range(rows):
                here = lax.shift_right_logical(cell, 7) == origin + p
                accs = [
                    jnp.where(here, jnp.take_along_axis(facing[k][p, f], cell & 127, axis=1), accs[f])
                    for f in range(F)
                ]
        picked.append(accs)
    for j in range(rows):
        for a in range(planes):
            base = (j * planes + a) * ITEMS
            for f in range(F):
                for g in range(F):
                    cells[base + f * F + g, 0:inst, :] = diag[a, j, f, g].astype(jnp.float32)
            for k in range(3):
                cells[base + LOWER + k, 0:inst, :] = coupling[k, a, j]
            side = coupling[2, a, j]
            for f in range(F):
                at = ((a * rows + j) * F + f) * LANES
                lower = left[a, f] if j == 0 else prev[a, j - 1, f]
                upper = right[a, f] if j == rows - 1 else prev[a, j + 1, f]
                value = source[a, j, f] + side * (lower + upper) - prod[0:inst, at : at + LANES]
                if a == planes - 1:
                    value = value - coupling[1, a, j] * picked[j][f]
                cells[base + SOURCE + f, 0:inst, :] = source[a, j, f]
                cells[base + RIGHT + f, 0:inst, :] = value
    flat = cells.reshape(count * HP, LANES)
    for h in range(HP):
        block = flat[pl.ds(h, count, stride=HP), :].T
        for d in range(n):
            turned[d, h // per_row, (h % per_row) * part : (h % per_row + 1) * part, :] = block[
                d * part : (d + 1) * part
            ]
    for d in range(n):
        for half in range(halves):
            block = turned[d, half].T
            for j in range(rows):
                out[d, j, half] = block[j * planes * ITEMS : (j + 1) * planes * ITEMS]


def reader(lines, group, planes):
    step = planes * ITEMS

    def read(a, k):
        return lines[pl.ds((a // planes) * group * step + (a % planes) * ITEMS + k, group, stride=step), :]

    return read


def sweep(read, right, last, group, fronts, emit):
    carried = [jnp.zeros((group, LANES), jnp.float32)] * F
    for a in range(last):
        lower = read(a, LOWER)
        vector = right(a)
        if a:
            vector = [vector[g] + lower * carried[g] for g in range(F)]
        carried = matvec(functools.partial(read, a), vector)
        if a < last - 1:
            for f in range(F):
                fronts[a, f] = carried[f]
    emit(last - 1, carried)
    for a in reversed(range(last - 1)):
        upper = read(a, UPPER)
        applied = matvec(functools.partial(read, a), carried)
        carried = [fronts[a, f] - upper * applied[f] for f in range(F)]
        emit(a, carried)


def first_kernel(planes, group, halves, lines, out, swapped, fronts):
    read = reader(lines, group, planes)
    last = lines.shape[0] // (group * planes * ITEMS) * planes

    def emit(a, values):
        for f in range(F):
            at = (a * F + f) * group
            out[at : at + group, :] = values[f]
            swapped[at : at + halves, :] = values[f][halves:]
            swapped[at + halves : at + group, :] = values[f][:halves]

    sweep(read, lambda a: [read(a, RIGHT + f) for f in range(F)], last, group, fronts, emit)


def second_kernel(
    planes, group, halves, part, azim, lines, value, swapped, from_left, from_right, spectral, face,
    crossed, partner, out, fronts, mix, spread, prod,
):
    read = reader(lines, group, planes)
    last = lines.shape[0] // (group * planes * ITEMS) * planes
    inst = spectral.shape[0]
    wide = halves * LANES
    mix[...] = jnp.zeros_like(mix)
    mix[0:inst, 0:inst] = spectral[...]
    lane = lax.broadcasted_iota(jnp.int32, (HP, wide), 1)
    instance = lax.broadcasted_iota(jnp.int32, (HP, wide), 0)
    shift = part.bit_length() - 1
    chosen = jnp.where(lax.shift_right_logical(lane, shift) == instance, 1.0, 0.0)
    over = lax.dot_general(
        mix[...], chosen, (((0,), (0,)), ((), ())), precision=HIGHEST, preferred_element_type=jnp.float32
    )
    over = lax.dot_general(
        chosen, over, (((0,), (0,)), ((), ())), precision=HIGHEST, preferred_element_type=jnp.float32
    )
    same = (lax.broadcasted_iota(jnp.int32, (wide, wide), 0) & (part - 1)) == (
        lax.broadcasted_iota(jnp.int32, (wide, wide), 1) & (part - 1)
    )
    spread[...] = jnp.where(same, over, 0.0)
    count = value.shape[0] // halves
    whole = jnp.concatenate(
        [value[pl.ds(half, count, stride=halves), :] for half in range(halves)], axis=1
    )
    mixed = jnp.dot(whole, spread[...], precision=HIGHEST, preferred_element_type=jnp.float32)
    for half in range(halves):
        prod[pl.ds(half, count, stride=halves), :] = mixed[:, half * LANES : (half + 1) * LANES]
    rows = group // halves
    count = F * group
    mine, axial = lax.axis_index("azim"), lax.axis_index("axial")
    owners = last // planes
    me = lax.rem(axial, owners)
    chip, core = lax.shift_right_logical(me, 1), me & 1
    lane_at = lax.broadcasted_iota(jnp.int32, (count, LANES), 1)
    row_cell = lax.broadcasted_iota(jnp.int32, (F, rows, halves, LANES), 1).reshape(count, LANES)
    cells, accs = [], []
    for j in range(rows):
        own = jnp.broadcast_to(face[j : j + 1, :], (count, LANES))
        cell = jnp.take_along_axis(own, me * part + (lane_at & (part - 1)), axis=1)
        cells.append((lax.shift_right_logical(cell, shift) - row_cell * owners, (lane_at & (LANES - part)) + (cell & (part - 1))))
        accs.append(jnp.zeros((count, LANES), jnp.float32))
    for side, buffer in enumerate((crossed, partner)):
        sender = core ^ side
        for k in range(buffer.shape[0]):
            for q in range(2):
                for i in range(azim):
                    owner = (chip ^ (2 * k + sender)) * 2 + (sender ^ q)
                    block = lax.rem(mine - i + azim, azim) * (rows * owners) + owner
                    values = buffer[k, q, i]
                    for j in range(rows):
                        accs[j] = jnp.where(
                            cells[j][0] == block, jnp.take_along_axis(values, cells[j][1], axis=1), accs[j]
                        )
    picked = [
        [
            sum(accs[j][(f * rows + p) * halves : (f * rows + p + 1) * halves] for p in range(rows))
            for f in range(F)
        ]
        for j in range(rows)
    ]
    first = lax.broadcasted_iota(jnp.int32, (group, LANES), 0) < halves

    def right(a):
        side = read(a, SIDE)
        result = []
        for f in range(F):
            at = (a * F + f) * group
            halo = jnp.where(first, from_left[at : at + group, :], from_right[at : at + group, :])
            around = swapped[at : at + group, :] + halo
            entry = read(a, SOURCE + f) + side * around - prod[at : at + group, :]
            if a == last - 1:
                face_rows = jnp.concatenate([picked[j][f] for j in range(rows)], axis=0)
                entry = entry - read(a, UPPER) * face_rows
            result.append(entry)
        return result

    def emit(a, values):
        for f in range(F):
            at = (a * F + f) * group
            out[at : at + group, :] = values[f]

    sweep(read, right, last, group, fronts, emit)


def unpack_kernel(halves, part, value, out, turned):
    n, count, _ = value.shape
    planes, rows, _, inst, _ = out.shape
    per_row = LANES // part
    for d in range(n):
        block = value[d].T
        for h8 in range(per_row):
            turned[h8, d * part : (d + 1) * part, :] = block[h8 * part : (h8 + 1) * part]
    for h8 in range(per_row):
        block = turned[h8].T
        for a in range(planes):
            for f in range(F):
                for j in range(rows):
                    for half in range(halves):
                        h = half * per_row + h8
                        at = ((a * F + f) * rows + j) * halves + half
                        if h < inst:
                            out[a, j, f, h : h + 1, :] = block[at : at + 1]


def shards(adjoint_source, adjoint_prev, diag_inverse, coupling, spectral, face_map):
    n, azim = lax.axis_size("axial") // 2, lax.axis_size("azim")
    planes, rows, _, inst, radial = adjoint_source.shape
    part = radial // n
    halves = HP * part // LANES
    group = rows * halves
    axial = [list(range(n)), list(range(n, 2 * n))]
    both = ("axial", "azim")
    f32 = jnp.float32
    last = n * planes

    def around(up, down):
        forward = [(i, (i + 1) % azim) for i in range(azim)]
        backward = [((i + 1) % azim, i) for i in range(azim)]
        if azim == 2 and up is down:
            got = lax.ppermute(up, "azim", forward)
            return got, got
        return lax.ppermute(up, "azim", forward), lax.ppermute(down, "azim", backward)

    face = face_map.reshape(rows, radial)
    if azim == 2:
        other, _ = around(adjoint_prev, adjoint_prev)
        left, right = other[:, rows - 1], other[:, 0]
    else:
        left, right = around(adjoint_prev[:, rows - 1], adjoint_prev[:, 0])
    facing = [
        lax.ppermute(
            adjoint_prev[0],
            both,
            [(n * azim + y, (n - 1) * azim + (y + k) % azim) for y in range(azim)],
        )
        for k in range(azim)
    ]
    count = rows * planes * ITEMS
    packed = pl.pallas_call(
        functools.partial(pack_kernel, n, azim),
        out_shape=jax.ShapeDtypeStruct((n, rows, halves, planes * ITEMS, LANES), f32),
        scratch_shapes=[
            pltpu.VMEM((count, HP, LANES), f32),
            pltpu.VMEM((n, halves, LANES, count), f32),
            pltpu.VMEM((HP, HP), f32),
            pltpu.VMEM((HP, planes * rows * F * LANES), f32),
        ],
        compiler_params=params(),
        name="pack",
    )(adjoint_source, adjoint_prev, left, right, diag_inverse, coupling, spectral, face, *facing)
    lines = lax.all_to_all(packed, "axial", 0, 0, axis_index_groups=axial, tiled=True)
    lines = lines.reshape(n * group * planes * ITEMS, LANES)
    shape = jax.ShapeDtypeStruct((last * F * group, LANES), f32)
    scratch = pltpu.VMEM((last, F, group, LANES), f32)
    value, swapped = pl.pallas_call(
        functools.partial(first_kernel, planes, group, halves),
        out_shape=(shape, shape),
        scratch_shapes=[scratch],
        compiler_params=params(),
        name="first_sweep",
    )(lines)
    from_left, from_right = around(swapped, swapped)
    piece = value[: F * group]
    pieces = [piece] + [
        lax.ppermute(piece, "azim", [(y, (y + k) % azim) for y in range(azim)]) for k in range(1, azim)
    ]
    piece = jnp.stack(pieces)
    core = [(i, i ^ 1) for i in range(2 * n)]
    chip = jnp.stack([piece, lax.ppermute(piece, "axial", core)])
    chips = n // 2
    crossed = jnp.stack(
        [
            lax.ppermute(
                chip,
                "axial",
                [(n + 2 * c + b, 2 * (c ^ (2 * k + b)) + b) for c in range(chips) for b in range(2)],
            )
            for k in range(chips // 2)
        ]
    )
    partner = lax.ppermute(crossed, "axial", core)
    value = pl.pallas_call(
        functools.partial(second_kernel, planes, group, halves, part, azim),
        out_shape=shape,
        scratch_shapes=[
            scratch,
            pltpu.VMEM((HP, HP), f32),
            pltpu.VMEM((halves * LANES, halves * LANES), f32),
            pltpu.VMEM((last * F * group, LANES), f32),
        ],
        compiler_params=params(),
        name="second_sweep",
    )(lines, value, swapped, from_left, from_right, spectral, face, crossed, partner)
    value = lax.all_to_all(
        value.reshape(n, planes * F * group, LANES), "axial", 0, 0, axis_index_groups=axial, tiled=True
    )
    return pl.pallas_call(
        functools.partial(unpack_kernel, halves, part),
        out_shape=jax.ShapeDtypeStruct(adjoint_source.shape, f32),
        scratch_shapes=[pltpu.VMEM((LANES // part, LANES, planes * F * group), f32)],
        compiler_params=params(),
        name="unpack",
    )(value)


def solution(mesh):
    placed = (
        P("axial", "azim", None, None, None),
        P("axial", "azim", None, None, None),
        P("axial", "azim", None, None, None, None),
        P(None, "axial", "azim", None, None),
        P(),
        P("azim"),
    )
    return jax.shard_map(
        shards,
        mesh=mesh,
        in_specs=placed,
        out_specs=P("axial", "azim", None, None, None),
        check_vma=False,
    )
```

```python
import functools

import jax
import jax.numpy as jnp
from jax import lax
from jax.experimental import pallas as pl
from jax.experimental.pallas import tpu as pltpu
from jax.sharding import PartitionSpec as P

F = 5
HP = 16
LANES = 128
LOWER, UPPER, SIDE, SOURCE, ITEMS = 25, 26, 27, 28, 33
HIGHEST = lax.Precision.HIGHEST


def params():
    return pltpu.CompilerParams(vmem_limit_bytes=48 * 2**20)


def matvec(matrix, vector):
    out = []
    for f in range(F):
        terms = [matrix(f * F + g) * vector[g] for g in range(F)]
        out.append((terms[0] + terms[1]) + (terms[2] + terms[3]) + terms[4])
    return out


def turn(n, rows, size, cells, turned, emit):
    me = lax.rem(lax.axis_index("axial"), n)
    part = LANES // n
    per_row = LANES // part
    halves = HP // per_row
    count = rows * size
    flat = cells.reshape(count * HP, LANES)
    for h in range(HP):
        block = flat[pl.ds(h, count, stride=HP), :].T
        for d in range(n):
            turned[d, h // per_row, (h % per_row) * part : (h % per_row + 1) * part, :] = block[
                d * part : (d + 1) * part
            ]
    for k in range(n):
        for half in range(halves):
            block = turned[me ^ k, half].T
            for j in range(rows):
                at = (j * halves + half) * size
                emit(k, at, block[j * size : (j + 1) * size])


def pack_kernel(n, source_in, prev_in, diag_in, coupling_in, spectral_in, face_in, *rest):
    outs, (source, prev, coupling, spectral, face) = rest[:n], rest[n : n + 5]
    cells, turned, diag, sems = rest[n + 5 :]
    copies = [
        pltpu.make_async_copy(a, b, sems.at[i])
        for i, (a, b) in enumerate(
            (
                (diag_in, diag),
                (coupling_in, coupling),
                (source_in, source),
                (prev_in, prev),
                (spectral_in, spectral),
                (face_in, face),
            )
        )
    ]
    for copy in copies:
        copy.start()
    planes, _, inst, rows, _ = source.shape
    size = planes * ITEMS
    cells[:, HP - 1, :] = jnp.zeros((rows * size, LANES), jnp.float32)
    for copy in copies:
        copy.wait()
    for j in range(rows):
        for a in range(planes):
            base = (j * planes + a) * ITEMS
            for f in range(F):
                for g in range(F):
                    cells[base + f * F + g, 0:inst, :] = diag[a, f, g, :, j, :].astype(jnp.float32)
            for k in range(3):
                cells[base + LOWER + k, 0:inst, :] = coupling[k, a, :, j, :]
            for f in range(F):
                cells[base + SOURCE + f, 0:inst, :] = source[a, f, :, j, :]

    def emit(k, at, block):
        outs[k][at : at + size, :] = block

    turn(n, rows, size, cells, turned, emit)


def right_kernel(n, azim, source, prev, left, right, coupling, spectral, face, *rest):
    facing, outs = rest[:azim], rest[azim + n : azim + 2 * n]
    cells, turned, mix, prod, held, sems = rest[azim + 2 * n :]
    planes, _, inst, rows, _ = source.shape
    mine = lax.axis_index("azim")
    cells[:, HP - 1, :] = jnp.zeros((rows * planes * F, LANES), jnp.float32)
    mix[...] = jnp.zeros_like(mix)
    mix[0:inst, 0:inst] = spectral[...]
    prod[HP - 1 :, :] = jnp.zeros((1, prod.shape[1]), jnp.float32)
    for a in range(planes):
        for j in range(rows):
            for f in range(F):
                at = ((a * rows + j) * F + f) * LANES
                prod[0:inst, at : at + LANES] = prev[a, f, :, j, :]
    prod[...] = jnp.dot(mix[...], prod[...], precision=HIGHEST, preferred_element_type=jnp.float32)
    picked = []
    for j in range(rows):
        cell = jnp.broadcast_to(face[j : j + 1, :], (inst, LANES))
        accs = [jnp.zeros((inst, LANES), jnp.float32)] * F
        for k in range(azim):
            origin = lax.rem(mine - k + azim, azim) * rows
            for p in range(rows):
                here = lax.shift_right_logical(cell, 7) == origin + p
                accs = [
                    jnp.where(here, jnp.take_along_axis(facing[k][0, f, :, p, :], cell & 127, axis=1), accs[f])
                    for f in range(F)
                ]
        picked.append(accs)
    for j in range(rows):
        for a in range(planes):
            side = coupling[2, a, :, j, :]
            for f in range(F):
                at = ((a * rows + j) * F + f) * LANES
                lower = left[a, f, :, rows - 1, :] if j == 0 else prev[a, f, :, j - 1, :]
                upper = right[a, f, :, 0, :] if j == rows - 1 else prev[a, f, :, j + 1, :]
                value = source[a, f, :, j, :] + side * (lower + upper) - prod[0:inst, at : at + LANES]
                if a == planes - 1:
                    value = value - coupling[1, a, :, j, :] * picked[j][f]
                cells[(j * planes + a) * F + f, 0:inst, :] = value
    size, count = planes * F, held.shape[1]

    def emit(k, at, block):
        held[k, at : at + size, :] = block

    turn(n, rows, size, cells, turned, emit)
    copies = [
        pltpu.make_async_copy(
            held.at[k], outs[k].at[pl.ds(outs[k].shape[0] - count, count), :], sems.at[k]
        )
        for k in range(n)
    ]
    for copy in copies:
        copy.start()
    for copy in copies:
        copy.wait()


def reader(lines, group, planes, items):
    step = planes * items

    def read(a, k):
        return lines[pl.ds((a // planes) * group * step + (a % planes) * items + k, group, stride=step), :]

    return read


def sweep(read, right, last, group, fronts, emit):
    carried = [jnp.zeros((group, LANES), jnp.float32)] * F
    for a in range(last):
        lower = read(a, LOWER)
        vector = right(a)
        if a:
            vector = [vector[g] + lower * carried[g] for g in range(F)]
        carried = matvec(functools.partial(read, a), vector)
        if a < last - 1:
            for f in range(F):
                fronts[a, f] = carried[f]
    emit(last - 1, carried)
    for a in reversed(range(last - 1)):
        upper = read(a, UPPER)
        applied = matvec(functools.partial(read, a), carried)
        carried = [fronts[a, f] - upper * applied[f] for f in range(F)]
        emit(a, carried)


def first_kernel(planes, group, halves, order, *refs):
    n = len(order)
    blocks, (lines, out, swapped, right_lines, fronts) = refs[:n], refs[n:]
    me = lax.rem(lax.axis_index("axial"), n)
    start = 0
    for target in (lines, right_lines):
        size = target.shape[0] // n
        for k, block in zip(order, blocks):
            target[pl.ds(pl.multiple_of((me ^ k) * size, 8), size), :] = block[start : start + size]
        start += size
    read = reader(lines, group, planes, ITEMS)
    read_right = reader(right_lines, group, planes, F)

    def emit(a, values):
        for f in range(F):
            at = (a * F + f) * group
            out[at : at + group, :] = values[f]
            swapped[at : at + halves, :] = values[f][halves:]
            swapped[at + halves : at + group, :] = values[f][:halves]

    sweep(read, lambda a: [read_right(a, f) for f in range(F)], n * planes, group, fronts, emit)


def second_kernel(
    planes, group, halves, part, azim, lines, value, swapped, from_left, from_right, spectral, face,
    crossed, partner, out, fronts, mix, spread, prod,
):
    read = reader(lines, group, planes, ITEMS)
    last = lines.shape[0] // (group * planes * ITEMS) * planes
    inst = spectral.shape[0]
    wide = halves * LANES
    mix[...] = jnp.zeros_like(mix)
    mix[0:inst, 0:inst] = spectral[...]
    lane = lax.broadcasted_iota(jnp.int32, (HP, wide), 1)
    instance = lax.broadcasted_iota(jnp.int32, (HP, wide), 0)
    shift = part.bit_length() - 1
    chosen = jnp.where(lax.shift_right_logical(lane, shift) == instance, 1.0, 0.0)
    over = lax.dot_general(
        mix[...], chosen, (((0,), (0,)), ((), ())), precision=HIGHEST, preferred_element_type=jnp.float32
    )
    over = lax.dot_general(
        chosen, over, (((0,), (0,)), ((), ())), precision=HIGHEST, preferred_element_type=jnp.float32
    )
    same = (lax.broadcasted_iota(jnp.int32, (wide, wide), 0) & (part - 1)) == (
        lax.broadcasted_iota(jnp.int32, (wide, wide), 1) & (part - 1)
    )
    spread[...] = jnp.where(same, over, 0.0)
    count = value.shape[0] // halves
    whole = jnp.concatenate(
        [value[pl.ds(half, count, stride=halves), :] for half in range(halves)], axis=1
    )
    mixed = jnp.dot(whole, spread[...], precision=HIGHEST, preferred_element_type=jnp.float32)
    for half in range(halves):
        prod[pl.ds(half, count, stride=halves), :] = mixed[:, half * LANES : (half + 1) * LANES]
    rows = group // halves
    count = F * group
    mine, axial = lax.axis_index("azim"), lax.axis_index("axial")
    owners = last // planes
    me = lax.rem(axial, owners)
    chip, core = lax.shift_right_logical(me, 1), me & 1
    lane_at = lax.broadcasted_iota(jnp.int32, (count, LANES), 1)
    row_cell = lax.broadcasted_iota(jnp.int32, (F, rows, halves, LANES), 1).reshape(count, LANES)
    cells, accs = [], []
    for j in range(rows):
        own = jnp.broadcast_to(face[j : j + 1, :], (count, LANES))
        cell = jnp.take_along_axis(own, me * part + (lane_at & (part - 1)), axis=1)
        cells.append((lax.shift_right_logical(cell, shift) - row_cell * owners, (lane_at & (LANES - part)) + (cell & (part - 1))))
        accs.append(jnp.zeros((count, LANES), jnp.float32))
    for side, buffer in enumerate((crossed, partner)):
        sender = core ^ side
        for k in range(buffer.shape[0]):
            for q in range(2):
                for i in range(azim):
                    owner = (chip ^ (2 * k + sender)) * 2 + (sender ^ q)
                    block = lax.rem(mine - i + azim, azim) * (rows * owners) + owner
                    values = buffer[k, q, i]
                    for j in range(rows):
                        accs[j] = jnp.where(
                            cells[j][0] == block, jnp.take_along_axis(values, cells[j][1], axis=1), accs[j]
                        )
    picked = [
        [
            sum(accs[j][(f * rows + p) * halves : (f * rows + p + 1) * halves] for p in range(rows))
            for f in range(F)
        ]
        for j in range(rows)
    ]
    first = lax.broadcasted_iota(jnp.int32, (group, LANES), 0) < halves

    def right(a):
        side = read(a, SIDE)
        result = []
        for f in range(F):
            at = (a * F + f) * group
            halo = jnp.where(first, from_left[at : at + group, :], from_right[at : at + group, :])
            around = swapped[at : at + group, :] + halo
            entry = read(a, SOURCE + f) + side * around - prod[at : at + group, :]
            if a == last - 1:
                face_rows = jnp.concatenate([picked[j][f] for j in range(rows)], axis=0)
                entry = entry - read(a, UPPER) * face_rows
            result.append(entry)
        return result

    def emit(a, values):
        for f in range(F):
            at = (a * F + f) * group
            out[at : at + group, :] = values[f]

    sweep(read, right, last, group, fronts, emit)


def unpack_kernel(halves, part, value, out, turned, block):
    n, count, _ = value.shape
    planes, _, inst, rows, _ = out.shape
    per_row = LANES // part
    for d in range(n):
        part_rows = value[d].T
        for h8 in range(per_row):
            turned[h8, d * part : (d + 1) * part, :] = part_rows[h8 * part : (h8 + 1) * part]
    for h8 in range(per_row):
        block[h8] = turned[h8].T
        for a in range(planes):
            for f in range(F):
                for half in range(halves):
                    h = half * per_row + h8
                    at = (a * F + f) * rows * halves + half
                    if h < inst:
                        out[a, f, h] = block[h8, pl.ds(at, rows, stride=halves), :]


def shards(adjoint_source, adjoint_prev, diag_inverse, coupling, spectral, face_map):
    n, azim = lax.axis_size("axial") // 2, lax.axis_size("azim")
    planes, rows, _, inst, radial = adjoint_source.shape
    source = adjoint_source.transpose(0, 2, 3, 1, 4)
    prev = adjoint_prev.transpose(0, 2, 3, 1, 4)
    diag = diag_inverse.transpose(0, 2, 3, 4, 1, 5)
    coupling = coupling.transpose(0, 1, 3, 2, 4)
    part = radial // n
    halves = HP * part // LANES
    group = rows * halves
    axial = [list(range(n)), list(range(n, 2 * n))]
    both = ("axial", "azim")
    f32 = jnp.float32
    last = n * planes

    def around(up, down):
        forward = [(i, (i + 1) % azim) for i in range(azim)]
        backward = [((i + 1) % azim, i) for i in range(azim)]
        if azim == 2:
            got = lax.ppermute(up, "azim", forward)
            return got, got
        return lax.ppermute(up, "azim", forward), lax.ppermute(down, "azim", backward)

    size, count = planes * ITEMS, planes * F
    hbm, vmem = pl.BlockSpec(memory_space=pltpu.HBM), pl.BlockSpec(memory_space=pltpu.VMEM)

    def like(x, *lead):
        return jax.ShapeDtypeStruct(lead or x.shape, x.dtype)

    face = face_map.reshape(rows, radial)
    left, right = around(prev, prev)
    facing = [
        lax.ppermute(
            prev, both, [(n * azim + y, (n - 1) * azim + (y + k) % azim) for y in range(azim)]
        )
        for k in range(azim)
    ]
    size, count = planes * ITEMS, planes * F
    block = jax.ShapeDtypeStruct((group * (size + count), LANES), f32)
    hbm, vmem, anywhere = (
        pl.BlockSpec(memory_space=space) for space in (pltpu.HBM, pltpu.VMEM, pl.ANY)
    )

    def like(x):
        return jax.ShapeDtypeStruct(x.shape, x.dtype)

    inputs = (source, prev, diag, coupling, spectral, face)
    *packed, source, prev, coupling, spectral, face = pl.pallas_call(
        functools.partial(pack_kernel, n),
        in_specs=[hbm] * 6,
        out_shape=[block] * n + [like(x) for x in (source, prev, coupling, spectral, face)],
        scratch_shapes=[
            pltpu.VMEM((rows * size, HP, LANES), f32),
            pltpu.VMEM((n, halves, LANES, rows * size), f32),
            pltpu.VMEM(diag.shape, diag.dtype),
            pltpu.SemaphoreType.DMA((6,)),
        ],
        compiler_params=params(),
        name="pack",
    )(*(pltpu.with_memory_space_constraint(x, pltpu.HBM) for x in inputs))
    packed = pl.pallas_call(
        functools.partial(right_kernel, n, azim),
        in_specs=[vmem] * (7 + azim) + [anywhere] * n,
        out_specs=[anywhere] * n,
        out_shape=[block] * n,
        scratch_shapes=[
            pltpu.VMEM((rows * count, HP, LANES), f32),
            pltpu.VMEM((n, halves, LANES, rows * count), f32),
            pltpu.VMEM((HP, HP), f32),
            pltpu.VMEM((HP, rows * count * LANES), f32),
            pltpu.VMEM((n, group * count, LANES), f32),
            pltpu.SemaphoreType.DMA((n,)),
        ],
        input_output_aliases={7 + azim + k: k for k in range(n)},
        compiler_params=params(),
        name="right_side",
    )(source, prev, left, right, coupling, spectral, face, *facing, *packed)
    order = sorted(range(n), key=lambda k: (k & 1, -bin(k & ~1).count("1"), k))
    blocks = [
        lax.ppermute(packed[k], "axial", [(i, i ^ k) for i in range(2 * n)]) if k else packed[k]
        for k in order
    ]
    shape = jax.ShapeDtypeStruct((last * F * group, LANES), f32)
    scratch = pltpu.VMEM((last, F, group, LANES), f32)
    lines, value, swapped = pl.pallas_call(
        functools.partial(first_kernel, planes, group, halves, order),
        out_shape=(jax.ShapeDtypeStruct((n * group * size, LANES), f32), shape, shape),
        scratch_shapes=[pltpu.VMEM((n * group * count, LANES), f32), scratch],
        compiler_params=params(),
        name="first_sweep",
    )(*blocks)
    from_left, from_right = around(swapped, swapped)
    piece = value[: F * group]
    pieces = [piece] + [
        lax.ppermute(piece, "azim", [(y, (y + k) % azim) for y in range(azim)]) for k in range(1, azim)
    ]
    piece = jnp.stack(pieces)
    core = [(i, i ^ 1) for i in range(2 * n)]
    chip = jnp.stack([piece, lax.ppermute(piece, "axial", core)])
    chips = n // 2
    crossed = jnp.stack(
        [
            lax.ppermute(
                chip,
                "axial",
                [(n + 2 * c + b, 2 * (c ^ (2 * k + b)) + b) for c in range(chips) for b in range(2)],
            )
            for k in range(chips // 2)
        ]
    )
    partner = lax.ppermute(crossed, "axial", core)
    value = pl.pallas_call(
        functools.partial(second_kernel, planes, group, halves, part, azim),
        out_shape=shape,
        scratch_shapes=[
            scratch,
            pltpu.VMEM((HP, HP), f32),
            pltpu.VMEM((halves * LANES, halves * LANES), f32),
            pltpu.VMEM((last * F * group, LANES), f32),
        ],
        compiler_params=params(),
        name="second_sweep",
    )(lines, value, swapped, from_left, from_right, spectral, face, crossed, partner)
    value = lax.all_to_all(
        value.reshape(n, planes * F * group, LANES), "axial", 0, 0, axis_index_groups=axial, tiled=True
    )
    out = pl.pallas_call(
        functools.partial(unpack_kernel, halves, part),
        out_shape=jax.ShapeDtypeStruct(source.shape, f32),
        scratch_shapes=[
            pltpu.VMEM((LANES // part, LANES, planes * F * group), f32),
            pltpu.VMEM((LANES // part, planes * F * group, LANES), f32),
        ],
        compiler_params=params(),
        name="unpack",
    )(value)
    return out.transpose(0, 3, 1, 2, 4)


def solution(mesh):
    placed = (
        P("axial", "azim", None, None, None),
        P("axial", "azim", None, None, None),
        P("axial", "azim", None, None, None, None),
        P(None, "axial", "azim", None, None),
        P(),
        P("azim"),
    )
    return jax.shard_map(
        shards,
        mesh=mesh,
        in_specs=placed,
        out_specs=P("axial", "azim", None, None, None),
        check_vma=False,
    )
```

```python
import functools

import jax
import jax.numpy as jnp
from jax import lax
from jax.experimental import pallas as pl
from jax.experimental.pallas import tpu as pltpu
from jax.sharding import PartitionSpec as P

F = 5
HP = 16
LANES = 128
LOWER, UPPER, SIDE, SOURCE, ITEMS = 25, 26, 27, 28, 33
HIGHEST = lax.Precision.HIGHEST


def params():
    return pltpu.CompilerParams(vmem_limit_bytes=48 * 2**20)


def matvec(matrix, vector):
    out = []
    for f in range(F):
        terms = [matrix(f * F + g) * vector[g] for g in range(F)]
        out.append((terms[0] + terms[1]) + (terms[2] + terms[3]) + terms[4])
    return out


def turn(n, rows, size, cells, turned, emit):
    me = lax.rem(lax.axis_index("axial"), n)
    part = LANES // n
    per_row = LANES // part
    halves = HP // per_row
    count = rows * size
    flat = cells.reshape(count * HP, LANES)
    for h in range(HP):
        block = flat[pl.ds(h, count, stride=HP), :].T
        for d in range(n):
            turned[d, h // per_row, (h % per_row) * part : (h % per_row + 1) * part, :] = block[
                d * part : (d + 1) * part
            ]
    for k in range(n):
        for half in range(halves):
            block = turned[me ^ k, half].T
            for j in range(rows):
                at = (j * halves + half) * size
                emit(k, at, block[j * size : (j + 1) * size])


def fetch_kernel(*refs):
    count = len(refs) // 2
    sources, targets, sems = refs[: count - 1], refs[count - 1 : -1], refs[-1]
    pairs = list(zip(sources, targets)) + [(sources[1].at[0], targets[-1])]
    copies = [pltpu.make_async_copy(a, b, sems.at[i]) for i, (a, b) in enumerate(pairs)]
    for copy in copies:
        copy.start()
    for copy in copies:
        copy.wait()


def pack_kernel(n, source, prev, diag, coupling, spectral, *rest):
    outs, base = rest[:n], rest[n]
    cells, turned, mix, prod = rest[n + 1 :]
    planes, _, inst, rows, _ = source.shape
    size = planes * ITEMS
    cells[:, HP - 1, :] = jnp.zeros((rows * size, LANES), jnp.float32)
    for j in range(rows):
        for a in range(planes):
            start = (j * planes + a) * ITEMS
            for f in range(F):
                for g in range(F):
                    cells[start + f * F + g, 0:inst, :] = diag[a, f, g, :, j, :].astype(jnp.float32)
            for k in range(3):
                cells[start + LOWER + k, 0:inst, :] = coupling[k, a, :, j, :]
            for f in range(F):
                cells[start + SOURCE + f, 0:inst, :] = source[a, f, :, j, :]
    mix[...] = jnp.zeros_like(mix)
    mix[0:inst, 0:inst] = spectral[...]
    prod[HP - 1 :, :] = jnp.zeros((1, prod.shape[1]), jnp.float32)
    for a in range(planes):
        for j in range(rows):
            for f in range(F):
                at = ((j * planes + a) * F + f) * LANES
                prod[0:inst, at : at + LANES] = prev[a, f, :, j, :]
    mixed = jnp.dot(mix[...], prod[...], precision=HIGHEST, preferred_element_type=jnp.float32)
    for j in range(rows):
        for a in range(planes):
            for f in range(F):
                at = (j * planes + a) * F + f
                base[at, 0:inst, :] = (
                    source[a, f, :, j, :] - mixed[0:inst, at * LANES : (at + 1) * LANES]
                )
                base[at, HP - 1 :, :] = jnp.zeros((1, LANES), jnp.float32)

    def emit(k, at, block):
        outs[k][at : at + size, :] = block

    turn(n, rows, size, cells, turned, emit)


def right_kernel(n, azim, *refs):
    facing, (left, right, prev, coupling, base, face) = refs[:azim], refs[azim : azim + 6]
    outs, (cells, turned, held, sems) = refs[azim + 6 + n : azim + 6 + 2 * n], refs[azim + 6 + 2 * n :]
    planes, _, inst, rows, _ = prev.shape
    mine = lax.axis_index("azim")
    for j in range(rows):
        cell = jnp.broadcast_to(face[j : j + 1, :], (inst, LANES))
        picked = [jnp.zeros((inst, LANES), jnp.float32)] * F
        for k in range(azim):
            origin = lax.rem(mine - k + azim, azim) * rows
            for p in range(rows):
                here = lax.shift_right_logical(cell, 7) == origin + p
                picked = [
                    jnp.where(here, jnp.take_along_axis(facing[k][f, :, p, :], cell & 127, axis=1), picked[f])
                    for f in range(F)
                ]
        for a in range(planes):
            side = coupling[2, a, :, j, :]
            for f in range(F):
                lower = left[a, f, :, rows - 1, :] if j == 0 else prev[a, f, :, j - 1, :]
                upper = right[a, f, :, 0, :] if j == rows - 1 else prev[a, f, :, j + 1, :]
                at = (j * planes + a) * F + f
                value = base[at, 0:inst, :] + side * (lower + upper)
                if a == planes - 1:
                    value = value - coupling[1, a, :, j, :] * picked[f]
                cells[at, 0:inst, :] = value
                cells[at, HP - 1 :, :] = jnp.zeros((1, LANES), jnp.float32)
    size, count = planes * F, held.shape[1]

    def emit(k, at, block):
        held[k, at : at + size, :] = block

    turn(n, rows, size, cells, turned, emit)
    copies = [
        pltpu.make_async_copy(
            held.at[k], outs[k].at[pl.ds(outs[k].shape[0] - count, count), :], sems.at[k]
        )
        for k in range(n)
    ]
    for copy in copies:
        copy.start()
    for copy in copies:
        copy.wait()


def reader(lines, group, planes, items):
    step = planes * items

    def read(a, k):
        return lines[pl.ds((a // planes) * group * step + (a % planes) * items + k, group, stride=step), :]

    return read


def sweep(read, right, last, group, fronts, emit):
    carried = [jnp.zeros((group, LANES), jnp.float32)] * F
    for a in range(last):
        lower = read(a, LOWER)
        vector = right(a)
        if a:
            vector = [vector[g] + lower * carried[g] for g in range(F)]
        carried = matvec(functools.partial(read, a), vector)
        if a < last - 1:
            for f in range(F):
                fronts[a, f] = carried[f]
    emit(last - 1, carried)
    for a in reversed(range(last - 1)):
        upper = read(a, UPPER)
        applied = matvec(functools.partial(read, a), carried)
        carried = [fronts[a, f] - upper * applied[f] for f in range(F)]
        emit(a, carried)


def first_kernel(planes, group, halves, order, *refs):
    n = len(order)
    blocks, (lines, out, swapped, right_lines, fronts) = refs[:n], refs[n:]
    me = lax.rem(lax.axis_index("axial"), n)
    start = 0
    for target in (lines, right_lines):
        size = target.shape[0] // n
        for k, block in zip(order, blocks):
            target[pl.ds(pl.multiple_of((me ^ k) * size, 8), size), :] = block[start : start + size]
        start += size
    read = reader(lines, group, planes, ITEMS)
    read_right = reader(right_lines, group, planes, F)

    def emit(a, values):
        for f in range(F):
            at = (a * F + f) * group
            out[at : at + group, :] = values[f]
            swapped[at : at + halves, :] = values[f][halves:]
            swapped[at + halves : at + group, :] = values[f][:halves]

    sweep(read, lambda a: [read_right(a, f) for f in range(F)], n * planes, group, fronts, emit)


def middle_kernel(planes, group, halves, part, lines, value, swapped, spectral, out, mix, spread, prod):
    read = reader(lines, group, planes, ITEMS)
    inst = spectral.shape[0]
    wide = halves * LANES
    mix[...] = jnp.zeros_like(mix)
    mix[0:inst, 0:inst] = spectral[...]
    lane = lax.broadcasted_iota(jnp.int32, (HP, wide), 1)
    instance = lax.broadcasted_iota(jnp.int32, (HP, wide), 0)
    shift = part.bit_length() - 1
    chosen = jnp.where(lax.shift_right_logical(lane, shift) == instance, 1.0, 0.0)
    over = lax.dot_general(
        mix[...], chosen, (((0,), (0,)), ((), ())), precision=HIGHEST, preferred_element_type=jnp.float32
    )
    over = lax.dot_general(
        chosen, over, (((0,), (0,)), ((), ())), precision=HIGHEST, preferred_element_type=jnp.float32
    )
    same = (lax.broadcasted_iota(jnp.int32, (wide, wide), 0) & (part - 1)) == (
        lax.broadcasted_iota(jnp.int32, (wide, wide), 1) & (part - 1)
    )
    spread[...] = jnp.where(same, over, 0.0)
    count = value.shape[0] // halves
    whole = jnp.concatenate(
        [value[pl.ds(half, count, stride=halves), :] for half in range(halves)], axis=1
    )
    mixed = jnp.dot(whole, spread[...], precision=HIGHEST, preferred_element_type=jnp.float32)
    for half in range(halves):
        prod[pl.ds(half, count, stride=halves), :] = mixed[:, half * LANES : (half + 1) * LANES]
    for a in range(value.shape[0] // (F * group)):
        side = read(a, SIDE)
        for f in range(F):
            at = (a * F + f) * group
            out[at : at + group, :] = (
                read(a, SOURCE + f) + side * swapped[at : at + group, :] - prod[at : at + group, :]
            )


def second_kernel(planes, group, halves, part, azim, lines, ready, from_left, from_right, face, *rest):
    *pieces, out, fronts = rest
    crossed, partner = pieces[: len(pieces) // 2], pieces[len(pieces) // 2 :]
    read = reader(lines, group, planes, ITEMS)
    last = lines.shape[0] // (group * planes * ITEMS) * planes
    shift = part.bit_length() - 1
    rows = group // halves
    count = F * group
    mine, axial = lax.axis_index("azim"), lax.axis_index("axial")
    owners = last // planes
    me = lax.rem(axial, owners)
    chip, core = lax.shift_right_logical(me, 1), me & 1
    lane_at = lax.broadcasted_iota(jnp.int32, (count, LANES), 1)
    row_cell = lax.broadcasted_iota(jnp.int32, (F, rows, halves, LANES), 1).reshape(count, LANES)
    cells, accs = [], []
    for j in range(rows):
        own = jnp.broadcast_to(face[j : j + 1, :], (count, LANES))
        cell = jnp.take_along_axis(own, me * part + (lane_at & (part - 1)), axis=1)
        block = jnp.where(axial < owners, lax.shift_right_logical(cell, shift) - row_cell * owners, -1)
        cells.append((block, (lane_at & (LANES - part)) + (cell & (part - 1))))
        accs.append(jnp.zeros((count, LANES), jnp.float32))
    for side, buffers in enumerate((crossed, partner)):
        sender = core ^ side
        for at, buffer in enumerate(buffers):
            k, i = at // azim, at % azim
            for q in range(2):
                owner = (chip ^ (2 * k + sender)) * 2 + (sender ^ q)
                block = lax.rem(mine - i + azim, azim) * (rows * owners) + owner
                values = buffer[q]
                for j in range(rows):
                    accs[j] = jnp.where(
                        cells[j][0] == block, jnp.take_along_axis(values, cells[j][1], axis=1), accs[j]
                    )
    picked = [
        [
            sum(accs[j][(f * rows + p) * halves : (f * rows + p + 1) * halves] for p in range(rows))
            for f in range(F)
        ]
        for j in range(rows)
    ]
    first = lax.broadcasted_iota(jnp.int32, (group, LANES), 0) < halves

    def right(a):
        side = read(a, SIDE)
        result = []
        for f in range(F):
            at = (a * F + f) * group
            halo = jnp.where(first, from_left[at : at + group, :], from_right[at : at + group, :])
            entry = ready[at : at + group, :] + side * halo
            if a == last - 1:
                face_rows = jnp.concatenate([picked[j][f] for j in range(rows)], axis=0)
                entry = entry - read(a, UPPER) * face_rows
            result.append(entry)
        return result

    def emit(a, values):
        for f in range(F):
            at = (a * F + f) * group
            out[at : at + group, :] = values[f]

    sweep(read, right, last, group, fronts, emit)


def unpack_kernel(halves, part, value, out, turned, block):
    n, count, _ = value.shape
    planes, _, inst, rows, _ = out.shape
    per_row = LANES // part
    for d in range(n):
        part_rows = value[d].T
        for h8 in range(per_row):
            turned[h8, d * part : (d + 1) * part, :] = part_rows[h8 * part : (h8 + 1) * part]
    for h8 in range(per_row):
        block[h8] = turned[h8].T
        for a in range(planes):
            for f in range(F):
                for half in range(halves):
                    h = half * per_row + h8
                    at = (a * F + f) * rows * halves + half
                    if h < inst:
                        out[a, f, h] = block[h8, pl.ds(at, rows, stride=halves), :]


def shards(adjoint_source, adjoint_prev, diag_inverse, coupling, spectral, face_map):
    n, azim = lax.axis_size("axial") // 2, lax.axis_size("azim")
    planes, rows, _, inst, radial = adjoint_source.shape
    source = adjoint_source.transpose(0, 2, 3, 1, 4)
    prev = adjoint_prev.transpose(0, 2, 3, 1, 4)
    diag = diag_inverse.transpose(0, 2, 3, 4, 1, 5)
    coupling = coupling.transpose(0, 1, 3, 2, 4)
    part = radial // n
    halves = HP * part // LANES
    group = rows * halves
    axial = [list(range(n)), list(range(n, 2 * n))]
    both = ("axial", "azim")
    f32 = jnp.float32
    last = n * planes

    def around(up, down):
        forward = [(i, (i + 1) % azim) for i in range(azim)]
        backward = [((i + 1) % azim, i) for i in range(azim)]
        if azim == 2:
            got = lax.ppermute(up, "azim", forward)
            return got, got
        return lax.ppermute(up, "azim", forward), lax.ppermute(down, "azim", backward)

    size, count = planes * ITEMS, planes * F
    hbm, vmem = pl.BlockSpec(memory_space=pltpu.HBM), pl.BlockSpec(memory_space=pltpu.VMEM)

    def like(x, *lead):
        return jax.ShapeDtypeStruct(lead or x.shape, x.dtype)

    face = face_map.reshape(rows, radial)
    size, count = planes * ITEMS, planes * F
    block = jax.ShapeDtypeStruct((group * (size + count), LANES), f32)
    hbm, vmem, anywhere = (
        pl.BlockSpec(memory_space=space) for space in (pltpu.HBM, pltpu.VMEM, pl.ANY)
    )
    inputs = (source, prev, diag, coupling, spectral, face)
    source, prev, diag, coupling, spectral, face, first = pl.pallas_call(
        fetch_kernel,
        in_specs=[hbm] * 6,
        out_shape=[jax.ShapeDtypeStruct(x.shape, x.dtype) for x in inputs]
        + [jax.ShapeDtypeStruct(prev.shape[1:], f32)],
        scratch_shapes=[pltpu.SemaphoreType.DMA((7,))],
        compiler_params=params(),
        name="fetch",
    )(*(pltpu.with_memory_space_constraint(x, pltpu.HBM) for x in inputs))
    left, right = around(prev, prev)
    facing = [
        lax.ppermute(
            first, both, [(n * azim + y, (n - 1) * azim + (y + k) % azim) for y in range(azim)]
        )
        for k in range(azim)
    ]
    *packed, base = pl.pallas_call(
        functools.partial(pack_kernel, n),
        out_shape=[block] * n + [jax.ShapeDtypeStruct((rows * count, HP, LANES), f32)],
        scratch_shapes=[
            pltpu.VMEM((rows * size, HP, LANES), f32),
            pltpu.VMEM((n, halves, LANES, rows * size), f32),
            pltpu.VMEM((HP, HP), f32),
            pltpu.VMEM((HP, rows * count * LANES), f32),
        ],
        compiler_params=params(),
        name="pack",
    )(source, prev, diag, coupling, spectral)
    packed = pl.pallas_call(
        functools.partial(right_kernel, n, azim),
        in_specs=[vmem] * (6 + azim) + [anywhere] * n,
        out_specs=[anywhere] * n,
        out_shape=[block] * n,
        scratch_shapes=[
            pltpu.VMEM((rows * count, HP, LANES), f32),
            pltpu.VMEM((n, halves, LANES, rows * count), f32),
            pltpu.VMEM((n, group * count, LANES), f32),
            pltpu.SemaphoreType.DMA((n,)),
        ],
        input_output_aliases={6 + azim + k: k for k in range(n)},
        compiler_params=params(),
        name="right_side",
    )(*facing, left, right, prev, coupling, base, face, *packed)
    order = sorted(range(n), key=lambda k: (k & 1, -bin(k & ~1).count("1"), k))
    blocks = [
        lax.ppermute(packed[k], "axial", [(i, i ^ k) for i in range(2 * n)]) if k else packed[k]
        for k in order
    ]
    shape = jax.ShapeDtypeStruct((last * F * group, LANES), f32)
    scratch = pltpu.VMEM((last, F, group, LANES), f32)
    lines, value, swapped = pl.pallas_call(
        functools.partial(first_kernel, planes, group, halves, order),
        out_shape=(jax.ShapeDtypeStruct((n * group * size, LANES), f32), shape, shape),
        scratch_shapes=[pltpu.VMEM((n * group * count, LANES), f32), scratch],
        compiler_params=params(),
        name="first_sweep",
    )(*blocks)
    from_left, from_right = around(swapped, swapped)
    piece = value[: F * group]
    core = [(i, i ^ 1) for i in range(2 * n)]
    chip = jnp.stack([piece, lax.ppermute(piece, "axial", core)])
    chips = n // 2
    crossed = []
    for k in range(chips // 2):
        for i in range(azim):
            there = [
                ((n + 2 * c + b) * azim + y, (2 * (c ^ (2 * k + b)) + b) * azim + (y + i) % azim)
                for c in range(chips)
                for b in range(2)
                for y in range(azim)
            ]
            crossed.append(lax.ppermute(chip, both, there + [(b, a) for a, b in there]))
    partner = [lax.ppermute(x, "axial", core) for x in crossed]
    ready = pl.pallas_call(
        functools.partial(middle_kernel, planes, group, halves, part),
        out_shape=shape,
        scratch_shapes=[
            pltpu.VMEM((HP, HP), f32),
            pltpu.VMEM((halves * LANES, halves * LANES), f32),
            pltpu.VMEM((last * F * group, LANES), f32),
        ],
        compiler_params=params(),
        name="spectral_term",
    )(lines, value, swapped, spectral)
    value = pl.pallas_call(
        functools.partial(second_kernel, planes, group, halves, part, azim),
        out_shape=shape,
        scratch_shapes=[scratch],
        compiler_params=params(),
        name="second_sweep",
    )(lines, ready, from_left, from_right, face, *crossed, *partner)
    value = lax.all_to_all(
        value.reshape(n, planes * F * group, LANES), "axial", 0, 0, axis_index_groups=axial, tiled=True
    )
    out = pl.pallas_call(
        functools.partial(unpack_kernel, halves, part),
        out_shape=jax.ShapeDtypeStruct(source.shape, f32),
        scratch_shapes=[
            pltpu.VMEM((LANES // part, LANES, planes * F * group), f32),
            pltpu.VMEM((LANES // part, planes * F * group, LANES), f32),
        ],
        compiler_params=params(),
        name="unpack",
    )(value)
    return out.transpose(0, 3, 1, 2, 4)


def solution(mesh):
    placed = (
        P("axial", "azim", None, None, None),
        P("axial", "azim", None, None, None),
        P("axial", "azim", None, None, None, None),
        P(None, "axial", "azim", None, None),
        P(),
        P("azim"),
    )
    return jax.shard_map(
        shards,
        mesh=mesh,
        in_specs=placed,
        out_specs=P("axial", "azim", None, None, None),
        check_vma=False,
    )
```

```python
import functools

import jax
import jax.numpy as jnp
from jax import lax
from jax.experimental import pallas as pl
from jax.experimental.pallas import tpu as pltpu
from jax.sharding import PartitionSpec as P

F = 5
HP = 16
LANES = 128
LOWER, UPPER, SIDE, SOURCE, ITEMS = 25, 26, 27, 28, 33
HIGHEST = lax.Precision.HIGHEST


def params():
    return pltpu.CompilerParams(vmem_limit_bytes=48 * 2**20)


def matvec(matrix, vector):
    out = []
    for f in range(F):
        terms = [matrix(f * F + g) * vector[g] for g in range(F)]
        out.append((terms[0] + terms[1]) + (terms[2] + terms[3]) + terms[4])
    return out


def turn(n, rows, size, cells, turned, emit):
    me = lax.rem(lax.axis_index("axial"), n)
    part = LANES // n
    per_row = LANES // part
    halves = HP // per_row
    count = rows * size
    flat = cells.reshape(count * HP, LANES)
    for h in range(HP):
        block = flat[pl.ds(h, count, stride=HP), :].T
        for d in range(n):
            turned[d, h // per_row, (h % per_row) * part : (h % per_row + 1) * part, :] = block[
                d * part : (d + 1) * part
            ]
    for k in range(n):
        for half in range(halves):
            block = turned[me ^ k, half].T
            for j in range(rows):
                at = (j * halves + half) * size
                emit(k, at, block[j * size : (j + 1) * size])


def fetch_kernel(*refs):
    count = len(refs) // 2
    sources, targets, sems = refs[: count - 1], refs[count - 1 : -1], refs[-1]
    pairs = list(zip(sources, targets)) + [(sources[1].at[0], targets[-1])]
    copies = [pltpu.make_async_copy(a, b, sems.at[i]) for i, (a, b) in enumerate(pairs)]
    for copy in copies:
        copy.start()
    for copy in copies:
        copy.wait()


def pack_kernel(n, source, prev, diag, coupling, spectral, *rest):
    outs, base = rest[:n], rest[n]
    cells, turned, mix, prod = rest[n + 1 :]
    planes, _, inst, rows, _ = source.shape
    size = planes * ITEMS
    cells[:, HP - 1, :] = jnp.zeros((rows * size, LANES), jnp.float32)
    for j in range(rows):
        for a in range(planes):
            start = (j * planes + a) * ITEMS
            for f in range(F):
                for g in range(F):
                    cells[start + f * F + g, 0:inst, :] = diag[a, f, g, :, j, :].astype(jnp.float32)
            for k in range(3):
                cells[start + LOWER + k, 0:inst, :] = coupling[k, a, :, j, :]
            for f in range(F):
                cells[start + SOURCE + f, 0:inst, :] = source[a, f, :, j, :]
    mix[...] = jnp.zeros_like(mix)
    mix[0:inst, 0:inst] = spectral[...]
    prod[HP - 1 :, :] = jnp.zeros((1, prod.shape[1]), jnp.float32)
    for a in range(planes):
        for j in range(rows):
            for f in range(F):
                at = ((j * planes + a) * F + f) * LANES
                prod[0:inst, at : at + LANES] = prev[a, f, :, j, :]
    mixed = jnp.dot(mix[...], prod[...], precision=HIGHEST, preferred_element_type=jnp.float32)
    for j in range(rows):
        for a in range(planes):
            for f in range(F):
                at = (j * planes + a) * F + f
                base[at, 0:inst, :] = (
                    source[a, f, :, j, :] - mixed[0:inst, at * LANES : (at + 1) * LANES]
                )
                base[at, HP - 1 :, :] = jnp.zeros((1, LANES), jnp.float32)

    def emit(k, at, block):
        outs[k][at : at + size, :] = block

    turn(n, rows, size, cells, turned, emit)


def right_kernel(n, azim, *refs):
    facing, (left, right, prev, coupling, base, face) = refs[:azim], refs[azim : azim + 6]
    outs, (cells, turned, held, sems) = refs[azim + 6 + n : azim + 6 + 2 * n], refs[azim + 6 + 2 * n :]
    planes, _, inst, rows, _ = prev.shape
    mine = lax.axis_index("azim")
    for j in range(rows):
        cell = jnp.broadcast_to(face[j : j + 1, :], (inst, LANES))
        picked = [jnp.zeros((inst, LANES), jnp.float32)] * F
        for k in range(azim):
            origin = lax.rem(mine - k + azim, azim) * rows
            for p in range(rows):
                here = lax.shift_right_logical(cell, 7) == origin + p
                picked = [
                    jnp.where(here, jnp.take_along_axis(facing[k][f, :, p, :], cell & 127, axis=1), picked[f])
                    for f in range(F)
                ]
        for a in range(planes):
            side = coupling[2, a, :, j, :]
            for f in range(F):
                lower = left[a, f, :, rows - 1, :] if j == 0 else prev[a, f, :, j - 1, :]
                upper = right[a, f, :, 0, :] if j == rows - 1 else prev[a, f, :, j + 1, :]
                at = (j * planes + a) * F + f
                value = base[at, 0:inst, :] + side * (lower + upper)
                if a == planes - 1:
                    value = value - coupling[1, a, :, j, :] * picked[f]
                cells[at, 0:inst, :] = value
                cells[at, HP - 1 :, :] = jnp.zeros((1, LANES), jnp.float32)
    size, count = planes * F, held.shape[1]

    def emit(k, at, block):
        held[k, at : at + size, :] = block

    turn(n, rows, size, cells, turned, emit)
    copies = [
        pltpu.make_async_copy(
            held.at[k], outs[k].at[pl.ds(outs[k].shape[0] - count, count), :], sems.at[k]
        )
        for k in range(n)
    ]
    for copy in copies:
        copy.start()
    for copy in copies:
        copy.wait()


def reader(lines, group, planes, items):
    step = planes * items

    def read(a, k):
        return lines[pl.ds((a // planes) * group * step + (a % planes) * items + k, group, stride=step), :]

    return read


def forward(read, right, last, group, fronts):
    carried = [jnp.zeros((group, LANES), jnp.float32)] * F
    for a in range(last):
        vector = right(a)
        if a:
            lower = read(a, LOWER)
            vector = [vector[g] + lower * carried[g] for g in range(F)]
        if a < last - 1:
            carried = matvec(functools.partial(read, a), vector)
            for f in range(F):
                fronts[a, f] = carried[f]
    return vector


def backward(read, vector, last, fronts, emit):
    carried = matvec(functools.partial(read, last - 1), vector)
    emit(last - 1, carried)
    for a in reversed(range(last - 1)):
        upper = read(a, UPPER)
        applied = matvec(functools.partial(read, a), carried)
        carried = [fronts[a, f] - upper * applied[f] for f in range(F)]
        emit(a, carried)


def first_kernel(planes, group, halves, order, *refs):
    n = len(order)
    blocks, (lines, out, swapped, right_lines, fronts) = refs[:n], refs[n:]
    me = lax.rem(lax.axis_index("axial"), n)
    start = 0
    for target in (lines, right_lines):
        size = target.shape[0] // n
        for k, block in zip(order, blocks):
            target[pl.ds(pl.multiple_of((me ^ k) * size, 8), size), :] = block[start : start + size]
        start += size
    read = reader(lines, group, planes, ITEMS)
    read_right = reader(right_lines, group, planes, F)

    def emit(a, values):
        for f in range(F):
            at = (a * F + f) * group
            out[at : at + group, :] = values[f]
            swapped[at : at + halves, :] = values[f][halves:]
            swapped[at + halves : at + group, :] = values[f][:halves]

    last = n * planes
    vector = forward(read, lambda a: [read_right(a, f) for f in range(F)], last, group, fronts)
    backward(read, vector, last, fronts, emit)


def middle_kernel(
    planes, group, halves, part, lines, value, swapped, spectral, ready, mix, spread, prod
):
    read = reader(lines, group, planes, ITEMS)
    inst = spectral.shape[0]
    wide = halves * LANES
    mix[...] = jnp.zeros_like(mix)
    mix[0:inst, 0:inst] = spectral[...]
    lane = lax.broadcasted_iota(jnp.int32, (HP, wide), 1)
    instance = lax.broadcasted_iota(jnp.int32, (HP, wide), 0)
    shift = part.bit_length() - 1
    chosen = jnp.where(lax.shift_right_logical(lane, shift) == instance, 1.0, 0.0)
    over = lax.dot_general(
        mix[...], chosen, (((0,), (0,)), ((), ())), precision=HIGHEST, preferred_element_type=jnp.float32
    )
    over = lax.dot_general(
        chosen, over, (((0,), (0,)), ((), ())), precision=HIGHEST, preferred_element_type=jnp.float32
    )
    same = (lax.broadcasted_iota(jnp.int32, (wide, wide), 0) & (part - 1)) == (
        lax.broadcasted_iota(jnp.int32, (wide, wide), 1) & (part - 1)
    )
    spread[...] = jnp.where(same, over, 0.0)
    count = value.shape[0] // halves
    whole = jnp.concatenate(
        [value[pl.ds(half, count, stride=halves), :] for half in range(halves)], axis=1
    )
    mixed = jnp.dot(whole, spread[...], precision=HIGHEST, preferred_element_type=jnp.float32)
    for half in range(halves):
        prod[pl.ds(half, count, stride=halves), :] = mixed[:, half * LANES : (half + 1) * LANES]
    for a in range(value.shape[0] // (F * group)):
        side = read(a, SIDE)
        for f in range(F):
            at = (a * F + f) * group
            ready[at : at + group, :] = (
                read(a, SOURCE + f) + side * swapped[at : at + group, :] - prod[at : at + group, :]
            )


def collect_kernel(waited, *refs):
    *pieces, out = refs
    for i, piece in enumerate(pieces):
        out[i] = piece[...]


def second_kernel(
    planes, group, halves, part, azim, lines, ready, from_left, from_right, face, crossed, partner,
    out, fronts,
):
    read = reader(lines, group, planes, ITEMS)
    last = lines.shape[0] // (group * planes * ITEMS) * planes
    shift = part.bit_length() - 1
    rows = group // halves
    count = F * group
    mine, axial = lax.axis_index("azim"), lax.axis_index("axial")
    owners = last // planes
    me = lax.rem(axial, owners)
    chip, core = lax.shift_right_logical(me, 1), me & 1
    lane_at = lax.broadcasted_iota(jnp.int32, (count, LANES), 1)
    row_cell = lax.broadcasted_iota(jnp.int32, (F, rows, halves, LANES), 1).reshape(count, LANES)
    cells, accs = [], []
    for j in range(rows):
        own = jnp.broadcast_to(face[j : j + 1, :], (count, LANES))
        cell = jnp.take_along_axis(own, me * part + (lane_at & (part - 1)), axis=1)
        block = jnp.where(axial < owners, lax.shift_right_logical(cell, shift) - row_cell * owners, -1)
        cells.append((block, (lane_at & (LANES - part)) + (cell & (part - 1))))
        accs.append(jnp.zeros((count, LANES), jnp.float32))
    for side, buffers in enumerate((crossed, partner)):
        sender = core ^ side
        for at in range(buffers.shape[0]):
            k, i = at // azim, at % azim
            for q in range(2):
                owner = (chip ^ (2 * k + sender)) * 2 + (sender ^ q)
                block = lax.rem(mine - i + azim, azim) * (rows * owners) + owner
                values = buffers[at, q]
                for j in range(rows):
                    accs[j] = jnp.where(
                        cells[j][0] == block, jnp.take_along_axis(values, cells[j][1], axis=1), accs[j]
                    )
    picked = [
        [
            sum(accs[j][(f * rows + p) * halves : (f * rows + p + 1) * halves] for p in range(rows))
            for f in range(F)
        ]
        for j in range(rows)
    ]
    first = lax.broadcasted_iota(jnp.int32, (group, LANES), 0) < halves

    def right(a):
        side = read(a, SIDE)
        result = []
        for f in range(F):
            at = (a * F + f) * group
            halo = jnp.where(first, from_left[at : at + group, :], from_right[at : at + group, :])
            entry = ready[at : at + group, :] + side * halo
            if a == last - 1:
                face_rows = jnp.concatenate([picked[j][f] for j in range(rows)], axis=0)
                entry = entry - read(a, UPPER) * face_rows
            result.append(entry)
        return result

    vector = forward(read, right, last, group, fronts)

    def emit(a, values):
        for f in range(F):
            at = (a * F + f) * group
            out[at : at + group, :] = values[f]

    backward(read, vector, last, fronts, emit)


def unpack_kernel(halves, part, value, out, turned, block):
    n, count, _ = value.shape
    planes, _, inst, rows, _ = out.shape
    per_row = LANES // part
    for d in range(n):
        part_rows = value[d].T
        for h8 in range(per_row):
            turned[h8, d * part : (d + 1) * part, :] = part_rows[h8 * part : (h8 + 1) * part]
    for h8 in range(per_row):
        block[h8] = turned[h8].T
        for a in range(planes):
            for f in range(F):
                for half in range(halves):
                    h = half * per_row + h8
                    at = (a * F + f) * rows * halves + half
                    if h < inst:
                        out[a, f, h] = block[h8, pl.ds(at, rows, stride=halves), :]


def shards(adjoint_source, adjoint_prev, diag_inverse, coupling, spectral, face_map):
    n, azim = lax.axis_size("axial") // 2, lax.axis_size("azim")
    planes, rows, _, inst, radial = adjoint_source.shape
    source = adjoint_source.transpose(0, 2, 3, 1, 4)
    prev = adjoint_prev.transpose(0, 2, 3, 1, 4)
    diag = diag_inverse.transpose(0, 2, 3, 4, 1, 5)
    coupling = coupling.transpose(0, 1, 3, 2, 4)
    part = radial // n
    halves = HP * part // LANES
    group = rows * halves
    axial = [list(range(n)), list(range(n, 2 * n))]
    both = ("axial", "azim")
    f32 = jnp.float32
    last = n * planes

    def around(up, down):
        forward = [(i, (i + 1) % azim) for i in range(azim)]
        backward = [((i + 1) % azim, i) for i in range(azim)]
        if azim == 2:
            got = lax.ppermute(up, "azim", forward)
            return got, got
        return lax.ppermute(up, "azim", forward), lax.ppermute(down, "azim", backward)

    size, count = planes * ITEMS, planes * F
    hbm, vmem = pl.BlockSpec(memory_space=pltpu.HBM), pl.BlockSpec(memory_space=pltpu.VMEM)

    def like(x, *lead):
        return jax.ShapeDtypeStruct(lead or x.shape, x.dtype)

    face = face_map.reshape(rows, radial)
    size, count = planes * ITEMS, planes * F
    block = jax.ShapeDtypeStruct((group * (size + count), LANES), f32)
    hbm, vmem, anywhere = (
        pl.BlockSpec(memory_space=space) for space in (pltpu.HBM, pltpu.VMEM, pl.ANY)
    )
    left, right = around(prev, prev)
    inputs = (source, prev, diag, coupling, spectral, face)
    source, prev, diag, coupling, spectral, face, first = pl.pallas_call(
        fetch_kernel,
        in_specs=[hbm] * 6,
        out_shape=[jax.ShapeDtypeStruct(x.shape, x.dtype) for x in inputs]
        + [jax.ShapeDtypeStruct(prev.shape[1:], f32)],
        scratch_shapes=[pltpu.SemaphoreType.DMA((7,))],
        compiler_params=params(),
        name="fetch",
    )(*(pltpu.with_memory_space_constraint(x, pltpu.HBM) for x in inputs))
    facing = [
        lax.ppermute(
            first, both, [(n * azim + y, (n - 1) * azim + (y + k) % azim) for y in range(azim)]
        )
        for k in range(azim)
    ]
    *packed, base = pl.pallas_call(
        functools.partial(pack_kernel, n),
        out_shape=[block] * n + [jax.ShapeDtypeStruct((rows * count, HP, LANES), f32)],
        scratch_shapes=[
            pltpu.VMEM((rows * size, HP, LANES), f32),
            pltpu.VMEM((n, halves, LANES, rows * size), f32),
            pltpu.VMEM((HP, HP), f32),
            pltpu.VMEM((HP, rows * count * LANES), f32),
        ],
        compiler_params=params(),
        name="pack",
    )(source, prev, diag, coupling, spectral)
    packed = pl.pallas_call(
        functools.partial(right_kernel, n, azim),
        in_specs=[vmem] * (6 + azim) + [anywhere] * n,
        out_specs=[anywhere] * n,
        out_shape=[block] * n,
        scratch_shapes=[
            pltpu.VMEM((rows * count, HP, LANES), f32),
            pltpu.VMEM((n, halves, LANES, rows * count), f32),
            pltpu.VMEM((n, group * count, LANES), f32),
            pltpu.SemaphoreType.DMA((n,)),
        ],
        input_output_aliases={6 + azim + k: k for k in range(n)},
        compiler_params=params(),
        name="right_side",
    )(*facing, left, right, prev, coupling, base, face, *packed)
    order = sorted(range(n), key=lambda k: (k & 1, -bin(k & ~1).count("1"), k))
    blocks = [
        lax.ppermute(packed[k], "axial", [(i, i ^ k) for i in range(2 * n)]) if k else packed[k]
        for k in order
    ]
    shape = jax.ShapeDtypeStruct((last * F * group, LANES), f32)
    scratch = pltpu.VMEM((last, F, group, LANES), f32)
    lines, value, swapped = pl.pallas_call(
        functools.partial(first_kernel, planes, group, halves, order),
        out_shape=(jax.ShapeDtypeStruct((n * group * size, LANES), f32), shape, shape),
        scratch_shapes=[pltpu.VMEM((n * group * count, LANES), f32), scratch],
        compiler_params=params(),
        name="first_sweep",
    )(*blocks)
    from_left, from_right = around(swapped, swapped)
    piece = value[: F * group]
    core = [(i, i ^ 1) for i in range(2 * n)]
    chip = jnp.stack([piece, lax.ppermute(piece, "axial", core)])
    chips = n // 2
    crossed = []
    for k in range(chips // 2):
        for i in range(azim):
            there = [
                ((n + 2 * c + b) * azim + y, (2 * (c ^ (2 * k + b)) + b) * azim + (y + i) % azim)
                for c in range(chips)
                for b in range(2)
                for y in range(azim)
            ]
            crossed.append(lax.ppermute(chip, both, there + [(b, a) for a, b in there]))
    ready = pl.pallas_call(
        functools.partial(middle_kernel, planes, group, halves, part),
        out_shape=shape,
        scratch_shapes=[
            pltpu.VMEM((HP, HP), f32),
            pltpu.VMEM((halves * LANES, halves * LANES), f32),
            pltpu.VMEM((last * F * group, LANES), f32),
        ],
        compiler_params=params(),
        name="spectral_term",
    )(lines, value, swapped, spectral)
    crossed = pl.pallas_call(
        collect_kernel,
        in_specs=[pl.BlockSpec(memory_space=pl.ANY)] + [vmem] * len(crossed),
        out_shape=jax.ShapeDtypeStruct((len(crossed),) + chip.shape, f32),
        compiler_params=params(),
        name="collect",
    )(ready, *crossed)
    partner = lax.ppermute(crossed, "axial", core)
    value = pl.pallas_call(
        functools.partial(second_kernel, planes, group, halves, part, azim),
        out_shape=shape,
        scratch_shapes=[scratch],
        compiler_params=params(),
        name="second_sweep",
    )(lines, ready, from_left, from_right, face, crossed, partner)
    value = lax.all_to_all(
        value.reshape(n, planes * F * group, LANES), "axial", 0, 0, axis_index_groups=axial, tiled=True
    )
    out = pl.pallas_call(
        functools.partial(unpack_kernel, halves, part),
        out_shape=jax.ShapeDtypeStruct(source.shape, f32),
        scratch_shapes=[
            pltpu.VMEM((LANES // part, LANES, planes * F * group), f32),
            pltpu.VMEM((LANES // part, planes * F * group, LANES), f32),
        ],
        compiler_params=params(),
        name="unpack",
    )(value)
    return out.transpose(0, 3, 1, 2, 4)


def solution(mesh):
    placed = (
        P("axial", "azim", None, None, None),
        P("axial", "azim", None, None, None),
        P("axial", "azim", None, None, None, None),
        P(None, "axial", "azim", None, None),
        P(),
        P("azim"),
    )
    return jax.shard_map(
        shards,
        mesh=mesh,
        in_specs=placed,
        out_specs=P("axial", "azim", None, None, None),
        check_vma=False,
    )
```

```python
import functools

import jax
import jax.numpy as jnp
from jax import lax
from jax.experimental import pallas as pl
from jax.experimental.pallas import tpu as pltpu
from jax.sharding import PartitionSpec as P

F = 5
HP = 16
LANES = 128
LOWER, UPPER, SIDE, SOURCE, ITEMS = 25, 26, 27, 28, 33
HIGHEST = lax.Precision.HIGHEST


def params():
    return pltpu.CompilerParams(vmem_limit_bytes=48 * 2**20)


def matvec(matrix, vector):
    out = []
    for f in range(F):
        terms = [matrix(f * F + g) * vector[g] for g in range(F)]
        out.append((terms[0] + terms[1]) + (terms[2] + terms[3]) + terms[4])
    return out


def turn(n, rows, size, cells, turned, emit):
    me = lax.rem(lax.axis_index("axial"), n)
    part = LANES // n
    per_row = LANES // part
    halves = HP // per_row
    count = rows * size
    flat = cells.reshape(count * HP, LANES)
    for h in range(HP):
        block = flat[pl.ds(h, count, stride=HP), :].T
        for d in range(n):
            turned[d, h // per_row, (h % per_row) * part : (h % per_row + 1) * part, :] = block[
                d * part : (d + 1) * part
            ]
    for k in range(n):
        for half in range(halves):
            block = turned[me ^ k, half].T
            for j in range(rows):
                at = (j * halves + half) * size
                emit(k, at, block[j * size : (j + 1) * size])


def fetch_kernel(*refs):
    count = len(refs) // 2
    sources, targets, sems = refs[: count - 1], refs[count - 1 : -1], refs[-1]
    pairs = list(zip(sources, targets)) + [(sources[1].at[0], targets[-1])]
    copies = [pltpu.make_async_copy(a, b, sems.at[i]) for i, (a, b) in enumerate(pairs)]
    for copy in copies:
        copy.start()
    for copy in copies:
        copy.wait()


def pack_kernel(n, source, prev, diag, coupling, spectral, *rest):
    outs, base = rest[:n], rest[n]
    cells, turned, mix, prod = rest[n + 1 :]
    planes, _, inst, rows, _ = source.shape
    size = planes * ITEMS
    cells[:, HP - 1, :] = jnp.zeros((rows * size, LANES), jnp.float32)
    for j in range(rows):
        for a in range(planes):
            start = (j * planes + a) * ITEMS
            for f in range(F):
                for g in range(F):
                    cells[start + f * F + g, 0:inst, :] = diag[a, f, g, :, j, :].astype(jnp.float32)
            for k in range(3):
                cells[start + LOWER + k, 0:inst, :] = coupling[k, a, :, j, :]
            for f in range(F):
                cells[start + SOURCE + f, 0:inst, :] = source[a, f, :, j, :]
    mix[...] = jnp.zeros_like(mix)
    mix[0:inst, 0:inst] = spectral[...]
    prod[HP - 1 :, :] = jnp.zeros((1, prod.shape[1]), jnp.float32)
    for a in range(planes):
        for j in range(rows):
            for f in range(F):
                at = ((j * planes + a) * F + f) * LANES
                prod[0:inst, at : at + LANES] = prev[a, f, :, j, :]
    mixed = jnp.dot(mix[...], prod[...], precision=HIGHEST, preferred_element_type=jnp.float32)
    for j in range(rows):
        for a in range(planes):
            for f in range(F):
                at = (j * planes + a) * F + f
                base[at, 0:inst, :] = (
                    source[a, f, :, j, :] - mixed[0:inst, at * LANES : (at + 1) * LANES]
                )
                base[at, HP - 1 :, :] = jnp.zeros((1, LANES), jnp.float32)

    def emit(k, at, block):
        outs[k][at : at + size, :] = block

    turn(n, rows, size, cells, turned, emit)


def right_kernel(n, azim, *refs):
    facing, (left, right, prev, coupling, base, face) = refs[:azim], refs[azim : azim + 6]
    packed, outs, (cells, turned) = refs[azim + 6 : -n - 2], refs[-n - 2 : -2], refs[-2:]
    planes, _, inst, rows, _ = prev.shape
    mine = lax.axis_index("azim")
    for j in range(rows):
        cell = jnp.broadcast_to(face[j : j + 1, :], (inst, LANES))
        picked = [jnp.zeros((inst, LANES), jnp.float32)] * F
        for k in range(azim):
            origin = lax.rem(mine - k + azim, azim) * rows
            for p in range(rows):
                here = lax.shift_right_logical(cell, 7) == origin + p
                picked = [
                    jnp.where(here, jnp.take_along_axis(facing[k][f, :, p, :], cell & 127, axis=1), picked[f])
                    for f in range(F)
                ]
        for a in range(planes):
            side = coupling[2, a, :, j, :]
            for f in range(F):
                lower = left[a, f, :, rows - 1, :] if j == 0 else prev[a, f, :, j - 1, :]
                upper = right[a, f, :, 0, :] if j == rows - 1 else prev[a, f, :, j + 1, :]
                at = (j * planes + a) * F + f
                value = base[at, 0:inst, :] + side * (lower + upper)
                if a == planes - 1:
                    value = value - coupling[1, a, :, j, :] * picked[f]
                cells[at, 0:inst, :] = value
                cells[at, HP - 1 :, :] = jnp.zeros((1, LANES), jnp.float32)
    size, before = planes * F, packed[0].shape[0]
    for k in range(n):
        outs[k][0:before, :] = packed[k][...]

    def emit(k, at, block):
        outs[k][before + at : before + at + size, :] = block

    turn(n, rows, size, cells, turned, emit)


def reader(lines, group, planes, items):
    step = planes * items

    def read(a, k):
        return lines[pl.ds((a // planes) * group * step + (a % planes) * items + k, group, stride=step), :]

    return read


def forward(read, right, last, group, fronts):
    carried = [jnp.zeros((group, LANES), jnp.float32)] * F
    for a in range(last):
        vector = right(a)
        if a:
            lower = read(a, LOWER)
            vector = [vector[g] + lower * carried[g] for g in range(F)]
        if a < last - 1:
            carried = matvec(functools.partial(read, a), vector)
            for f in range(F):
                fronts[a, f] = carried[f]
    return vector


def backward(read, vector, last, fronts, emit):
    carried = matvec(functools.partial(read, last - 1), vector)
    emit(last - 1, carried)
    for a in reversed(range(last - 1)):
        upper = read(a, UPPER)
        applied = matvec(functools.partial(read, a), carried)
        carried = [fronts[a, f] - upper * applied[f] for f in range(F)]
        emit(a, carried)


def first_kernel(planes, group, halves, order, *refs):
    n = len(order)
    blocks, (lines, out, swapped, right_lines, fronts) = refs[:n], refs[n:]
    me = lax.rem(lax.axis_index("axial"), n)
    start = 0
    for target in (lines, right_lines):
        size = target.shape[0] // n
        for k, block in zip(order, blocks):
            target[pl.ds(pl.multiple_of((me ^ k) * size, 8), size), :] = block[start : start + size]
        start += size
    read = reader(lines, group, planes, ITEMS)
    read_right = reader(right_lines, group, planes, F)

    def emit(a, values):
        for f in range(F):
            at = (a * F + f) * group
            out[at : at + group, :] = values[f]
            swapped[at : at + halves, :] = values[f][halves:]
            swapped[at + halves : at + group, :] = values[f][:halves]

    last = n * planes
    vector = forward(read, lambda a: [read_right(a, f) for f in range(F)], last, group, fronts)
    backward(read, vector, last, fronts, emit)


def middle_kernel(
    planes, group, halves, part, lines, value, swapped, spectral, ready, mix, spread, prod
):
    read = reader(lines, group, planes, ITEMS)
    inst = spectral.shape[0]
    wide = halves * LANES
    mix[...] = jnp.zeros_like(mix)
    mix[0:inst, 0:inst] = spectral[...]
    lane = lax.broadcasted_iota(jnp.int32, (HP, wide), 1)
    instance = lax.broadcasted_iota(jnp.int32, (HP, wide), 0)
    shift = part.bit_length() - 1
    chosen = jnp.where(lax.shift_right_logical(lane, shift) == instance, 1.0, 0.0)
    over = lax.dot_general(
        mix[...], chosen, (((0,), (0,)), ((), ())), precision=HIGHEST, preferred_element_type=jnp.float32
    )
    over = lax.dot_general(
        chosen, over, (((0,), (0,)), ((), ())), precision=HIGHEST, preferred_element_type=jnp.float32
    )
    same = (lax.broadcasted_iota(jnp.int32, (wide, wide), 0) & (part - 1)) == (
        lax.broadcasted_iota(jnp.int32, (wide, wide), 1) & (part - 1)
    )
    spread[...] = jnp.where(same, over, 0.0)
    count = value.shape[0] // halves
    whole = jnp.concatenate(
        [value[pl.ds(half, count, stride=halves), :] for half in range(halves)], axis=1
    )
    mixed = jnp.dot(whole, spread[...], precision=HIGHEST, preferred_element_type=jnp.float32)
    for half in range(halves):
        prod[pl.ds(half, count, stride=halves), :] = mixed[:, half * LANES : (half + 1) * LANES]
    for a in range(value.shape[0] // (F * group)):
        side = read(a, SIDE)
        for f in range(F):
            at = (a * F + f) * group
            ready[at : at + group, :] = (
                read(a, SOURCE + f) + side * swapped[at : at + group, :] - prod[at : at + group, :]
            )


def collect_kernel(waited, *refs):
    *pieces, out = refs
    for i, piece in enumerate(pieces):
        out[i] = piece[...]


def second_kernel(
    planes, group, halves, part, azim, lines, ready, from_left, from_right, face, crossed, partner,
    out, fronts,
):
    read = reader(lines, group, planes, ITEMS)
    last = lines.shape[0] // (group * planes * ITEMS) * planes
    shift = part.bit_length() - 1
    rows = group // halves
    count = F * group
    mine, axial = lax.axis_index("azim"), lax.axis_index("axial")
    owners = last // planes
    me = lax.rem(axial, owners)
    chip, core = lax.shift_right_logical(me, 1), me & 1
    lane_at = lax.broadcasted_iota(jnp.int32, (count, LANES), 1)
    row_cell = lax.broadcasted_iota(jnp.int32, (F, rows, halves, LANES), 1).reshape(count, LANES)
    cells, accs = [], []
    for j in range(rows):
        own = jnp.broadcast_to(face[j : j + 1, :], (count, LANES))
        cell = jnp.take_along_axis(own, me * part + (lane_at & (part - 1)), axis=1)
        block = jnp.where(axial < owners, lax.shift_right_logical(cell, shift) - row_cell * owners, -1)
        cells.append((block, (lane_at & (LANES - part)) + (cell & (part - 1))))
        accs.append(jnp.zeros((count, LANES), jnp.float32))
    for side, buffers in enumerate((crossed, partner)):
        sender = core ^ side
        for at in range(buffers.shape[0]):
            k, i = at // azim, at % azim
            for q in range(2):
                owner = (chip ^ (2 * k + sender)) * 2 + (sender ^ q)
                block = lax.rem(mine - i + azim, azim) * (rows * owners) + owner
                values = buffers[at, q]
                for j in range(rows):
                    accs[j] = jnp.where(
                        cells[j][0] == block, jnp.take_along_axis(values, cells[j][1], axis=1), accs[j]
                    )
    picked = [
        [
            sum(accs[j][(f * rows + p) * halves : (f * rows + p + 1) * halves] for p in range(rows))
            for f in range(F)
        ]
        for j in range(rows)
    ]
    first = lax.broadcasted_iota(jnp.int32, (group, LANES), 0) < halves

    def right(a):
        side = read(a, SIDE)
        result = []
        for f in range(F):
            at = (a * F + f) * group
            halo = jnp.where(first, from_left[at : at + group, :], from_right[at : at + group, :])
            entry = ready[at : at + group, :] + side * halo
            if a == last - 1:
                face_rows = jnp.concatenate([picked[j][f] for j in range(rows)], axis=0)
                entry = entry - read(a, UPPER) * face_rows
            result.append(entry)
        return result

    vector = forward(read, right, last, group, fronts)

    def emit(a, values):
        for f in range(F):
            at = (a * F + f) * group
            out[at : at + group, :] = values[f]

    backward(read, vector, last, fronts, emit)


def unpack_kernel(halves, part, value, out, turned, block):
    n, count, _ = value.shape
    planes, _, inst, rows, _ = out.shape
    per_row = LANES // part
    for d in range(n):
        part_rows = value[d].T
        for h8 in range(per_row):
            turned[h8, d * part : (d + 1) * part, :] = part_rows[h8 * part : (h8 + 1) * part]
    for h8 in range(per_row):
        block[h8] = turned[h8].T
        for a in range(planes):
            for f in range(F):
                for half in range(halves):
                    h = half * per_row + h8
                    at = (a * F + f) * rows * halves + half
                    if h < inst:
                        out[a, f, h] = block[h8, pl.ds(at, rows, stride=halves), :]


def shards(adjoint_source, adjoint_prev, diag_inverse, coupling, spectral, face_map):
    n, azim = lax.axis_size("axial") // 2, lax.axis_size("azim")
    planes, rows, _, inst, radial = adjoint_source.shape
    source = adjoint_source.transpose(0, 2, 3, 1, 4)
    prev = adjoint_prev.transpose(0, 2, 3, 1, 4)
    diag = diag_inverse.transpose(0, 2, 3, 4, 1, 5)
    coupling = coupling.transpose(0, 1, 3, 2, 4)
    part = radial // n
    halves = HP * part // LANES
    group = rows * halves
    axial = [list(range(n)), list(range(n, 2 * n))]
    both = ("axial", "azim")
    f32 = jnp.float32
    last = n * planes

    def around(up, down):
        forward = [(i, (i + 1) % azim) for i in range(azim)]
        backward = [((i + 1) % azim, i) for i in range(azim)]
        if azim == 2:
            got = lax.ppermute(up, "azim", forward)
            return got, got
        return lax.ppermute(up, "azim", forward), lax.ppermute(down, "azim", backward)

    size, count = planes * ITEMS, planes * F
    hbm, vmem = pl.BlockSpec(memory_space=pltpu.HBM), pl.BlockSpec(memory_space=pltpu.VMEM)

    def like(x, *lead):
        return jax.ShapeDtypeStruct(lead or x.shape, x.dtype)

    face = face_map.reshape(rows, radial)
    size, count = planes * ITEMS, planes * F
    block = jax.ShapeDtypeStruct((group * (size + count), LANES), f32)
    hbm, vmem = pl.BlockSpec(memory_space=pltpu.HBM), pl.BlockSpec(memory_space=pltpu.VMEM)
    left, right = around(prev, prev)
    inputs = (source, prev, diag, coupling, spectral, face)
    source, prev, diag, coupling, spectral, face, first = pl.pallas_call(
        fetch_kernel,
        in_specs=[hbm] * 6,
        out_shape=[jax.ShapeDtypeStruct(x.shape, x.dtype) for x in inputs]
        + [jax.ShapeDtypeStruct(prev.shape[1:], f32)],
        scratch_shapes=[pltpu.SemaphoreType.DMA((7,))],
        compiler_params=params(),
        name="fetch",
    )(*(pltpu.with_memory_space_constraint(x, pltpu.HBM) for x in inputs))
    facing = [
        lax.ppermute(
            first, both, [(n * azim + y, (n - 1) * azim + (y + k) % azim) for y in range(azim)]
        )
        for k in range(azim)
    ]
    *packed, base = pl.pallas_call(
        functools.partial(pack_kernel, n),
        out_shape=[jax.ShapeDtypeStruct((group * size, LANES), f32)] * n
        + [jax.ShapeDtypeStruct((rows * count, HP, LANES), f32)],
        scratch_shapes=[
            pltpu.VMEM((rows * size, HP, LANES), f32),
            pltpu.VMEM((n, halves, LANES, rows * size), f32),
            pltpu.VMEM((HP, HP), f32),
            pltpu.VMEM((HP, rows * count * LANES), f32),
        ],
        compiler_params=params(),
        name="pack",
    )(source, prev, diag, coupling, spectral)
    packed = pl.pallas_call(
        functools.partial(right_kernel, n, azim),
        out_shape=[block] * n,
        scratch_shapes=[
            pltpu.VMEM((rows * count, HP, LANES), f32),
            pltpu.VMEM((n, halves, LANES, rows * count), f32),
        ],
        compiler_params=params(),
        name="right_side",
    )(*facing, left, right, prev, coupling, base, face, *packed)
    order = sorted(range(n), key=lambda k: (k & 1, -bin(k & ~1).count("1"), k))
    blocks = [
        lax.ppermute(packed[k], "axial", [(i, i ^ k) for i in range(2 * n)]) if k else packed[k]
        for k in order
    ]
    shape = jax.ShapeDtypeStruct((last * F * group, LANES), f32)
    scratch = pltpu.VMEM((last, F, group, LANES), f32)
    lines, value, swapped = pl.pallas_call(
        functools.partial(first_kernel, planes, group, halves, order),
        out_shape=(jax.ShapeDtypeStruct((n * group * size, LANES), f32), shape, shape),
        scratch_shapes=[pltpu.VMEM((n * group * count, LANES), f32), scratch],
        compiler_params=params(),
        name="first_sweep",
    )(*blocks)
    from_left, from_right = around(swapped, swapped)
    piece = value[: F * group]
    core = [(i, i ^ 1) for i in range(2 * n)]
    chip = jnp.stack([piece, lax.ppermute(piece, "axial", core)])
    chips = n // 2
    crossed = []
    for k in range(chips // 2):
        for i in range(azim):
            there = [
                ((n + 2 * c + b) * azim + y, (2 * (c ^ (2 * k + b)) + b) * azim + (y + i) % azim)
                for c in range(chips)
                for b in range(2)
                for y in range(azim)
            ]
            crossed.append(lax.ppermute(chip, both, there + [(b, a) for a, b in there]))
    ready = pl.pallas_call(
        functools.partial(middle_kernel, planes, group, halves, part),
        out_shape=shape,
        scratch_shapes=[
            pltpu.VMEM((HP, HP), f32),
            pltpu.VMEM((halves * LANES, halves * LANES), f32),
            pltpu.VMEM((last * F * group, LANES), f32),
        ],
        compiler_params=params(),
        name="spectral_term",
    )(lines, value, swapped, spectral)
    crossed = pl.pallas_call(
        collect_kernel,
        in_specs=[pl.BlockSpec(memory_space=pl.ANY)] + [vmem] * len(crossed),
        out_shape=jax.ShapeDtypeStruct((len(crossed),) + chip.shape, f32),
        compiler_params=params(),
        name="collect",
    )(ready, *crossed)
    partner = lax.ppermute(crossed, "axial", core)
    value = pl.pallas_call(
        functools.partial(second_kernel, planes, group, halves, part, azim),
        out_shape=shape,
        scratch_shapes=[scratch],
        compiler_params=params(),
        name="second_sweep",
    )(lines, ready, from_left, from_right, face, crossed, partner)
    value = lax.all_to_all(
        value.reshape(n, planes * F * group, LANES), "axial", 0, 0, axis_index_groups=axial, tiled=True
    )
    out = pl.pallas_call(
        functools.partial(unpack_kernel, halves, part),
        out_shape=jax.ShapeDtypeStruct(source.shape, f32),
        scratch_shapes=[
            pltpu.VMEM((LANES // part, LANES, planes * F * group), f32),
            pltpu.VMEM((LANES // part, planes * F * group, LANES), f32),
        ],
        compiler_params=params(),
        name="unpack",
    )(value)
    return out.transpose(0, 3, 1, 2, 4)


def solution(mesh):
    placed = (
        P("axial", "azim", None, None, None),
        P("axial", "azim", None, None, None),
        P("axial", "azim", None, None, None, None),
        P(None, "axial", "azim", None, None),
        P(),
        P("azim"),
    )
    return jax.shard_map(
        shards,
        mesh=mesh,
        in_specs=placed,
        out_specs=P("axial", "azim", None, None, None),
        check_vma=False,
    )
```

```python
import functools

import jax
import jax.numpy as jnp
from jax import lax
from jax.experimental import pallas as pl
from jax.experimental.pallas import tpu as pltpu
from jax.sharding import PartitionSpec as P

F = 5
HP = 16
LANES = 128
LOWER, UPPER, SIDE, SOURCE, ITEMS = 25, 26, 27, 28, 33
HIGHEST = lax.Precision.HIGHEST


def params():
    return pltpu.CompilerParams(vmem_limit_bytes=48 * 2**20)


def matvec(matrix, vector):
    out = []
    for f in range(F):
        terms = [matrix(f * F + g) * vector[g] for g in range(F)]
        out.append((terms[0] + terms[1]) + (terms[2] + terms[3]) + terms[4])
    return out


def turn(n, rows, size, cells, turned, emit):
    me = lax.rem(lax.axis_index("axial"), n)
    part = LANES // n
    per_row = LANES // part
    halves = HP // per_row
    count = rows * size
    flat = cells.reshape(count * HP, LANES)
    for h in range(HP):
        block = flat[pl.ds(h, count, stride=HP), :].T
        for d in range(n):
            turned[d, h // per_row, (h % per_row) * part : (h % per_row + 1) * part, :] = block[
                d * part : (d + 1) * part
            ]
    for k in range(n):
        for half in range(halves):
            block = turned[me ^ k, half].T
            for j in range(rows):
                at = (j * halves + half) * size
                emit(k, at, block[j * size : (j + 1) * size])


def fetch_kernel(*refs):
    count = len(refs) // 2
    sources, targets, sems = refs[: count - 1], refs[count - 1 : -1], refs[-1]
    pairs = list(zip(sources, targets)) + [(sources[1].at[0], targets[-1])]
    copies = [pltpu.make_async_copy(a, b, sems.at[i]) for i, (a, b) in enumerate(pairs)]
    for copy in copies:
        copy.start()
    for copy in copies:
        copy.wait()


def pack_kernel(n, source, prev, diag, coupling, spectral, *rest):
    outs, base = rest[:n], rest[n]
    cells, turned, mix, prod = rest[n + 1 :]
    planes, _, inst, rows, _ = source.shape
    size = planes * ITEMS
    cells[:, HP - 1, :] = jnp.zeros((rows * size, LANES), jnp.float32)
    for j in range(rows):
        for a in range(planes):
            start = (j * planes + a) * ITEMS
            for f in range(F):
                for g in range(F):
                    cells[start + f * F + g, 0:inst, :] = diag[a, f, g, :, j, :].astype(jnp.float32)
            for k in range(3):
                cells[start + LOWER + k, 0:inst, :] = coupling[k, a, :, j, :]
            for f in range(F):
                cells[start + SOURCE + f, 0:inst, :] = source[a, f, :, j, :]
    mix[...] = jnp.zeros_like(mix)
    mix[0:inst, 0:inst] = spectral[...]
    prod[HP - 1 :, :] = jnp.zeros((1, prod.shape[1]), jnp.float32)
    for a in range(planes):
        for j in range(rows):
            for f in range(F):
                at = ((j * planes + a) * F + f) * LANES
                prod[0:inst, at : at + LANES] = prev[a, f, :, j, :]
    mixed = jnp.dot(mix[...], prod[...], precision=HIGHEST, preferred_element_type=jnp.float32)
    for j in range(rows):
        for a in range(planes):
            for f in range(F):
                at = (j * planes + a) * F + f
                base[at, 0:inst, :] = (
                    source[a, f, :, j, :] - mixed[0:inst, at * LANES : (at + 1) * LANES]
                )
                base[at, HP - 1 :, :] = jnp.zeros((1, LANES), jnp.float32)

    def emit(k, at, block):
        outs[k][at : at + size, :] = block

    turn(n, rows, size, cells, turned, emit)


def right_kernel(n, azim, *refs):
    facing, (left, right, prev, coupling, base, face) = refs[:azim], refs[azim : azim + 6]
    packed, outs, (cells, turned) = refs[azim + 6 : -n - 2], refs[-n - 2 : -2], refs[-2:]
    planes, _, inst, rows, _ = prev.shape
    mine = lax.axis_index("azim")
    for j in range(rows):
        cell = jnp.broadcast_to(face[j : j + 1, :], (inst, LANES))
        picked = [jnp.zeros((inst, LANES), jnp.float32)] * F
        for k in range(azim):
            origin = lax.rem(mine - k + azim, azim) * rows
            for p in range(rows):
                here = lax.shift_right_logical(cell, 7) == origin + p
                picked = [
                    jnp.where(here, jnp.take_along_axis(facing[k][f, :, p, :], cell & 127, axis=1), picked[f])
                    for f in range(F)
                ]
        for a in range(planes):
            side = coupling[2, a, :, j, :]
            for f in range(F):
                lower = left[a, f, :, rows - 1, :] if j == 0 else prev[a, f, :, j - 1, :]
                upper = right[a, f, :, 0, :] if j == rows - 1 else prev[a, f, :, j + 1, :]
                at = (j * planes + a) * F + f
                value = base[at, 0:inst, :] + side * (lower + upper)
                if a == planes - 1:
                    value = value - coupling[1, a, :, j, :] * picked[f]
                cells[at, 0:inst, :] = value
                cells[at, HP - 1 :, :] = jnp.zeros((1, LANES), jnp.float32)
    size, before = planes * F, packed[0].shape[0]
    for k in range(n):
        outs[k][0:before, :] = packed[k][...]

    def emit(k, at, block):
        outs[k][before + at : before + at + size, :] = block

    turn(n, rows, size, cells, turned, emit)


def reader(lines, group, planes, items):
    step = planes * items

    def read(a, k):
        return lines[pl.ds((a // planes) * group * step + (a % planes) * items + k, group, stride=step), :]

    return read


def forward(read, right, last, group, fronts):
    carried = [jnp.zeros((group, LANES), jnp.float32)] * F
    for a in range(last):
        vector = right(a)
        if a:
            lower = read(a, LOWER)
            vector = [vector[g] + lower * carried[g] for g in range(F)]
        if a < last - 1:
            carried = matvec(functools.partial(read, a), vector)
            for f in range(F):
                fronts[a, f] = carried[f]
    return vector


def backward(read, vector, last, fronts, emit):
    carried = matvec(functools.partial(read, last - 1), vector)
    emit(last - 1, carried)
    for a in reversed(range(last - 1)):
        upper = read(a, UPPER)
        applied = matvec(functools.partial(read, a), carried)
        carried = [fronts[a, f] - upper * applied[f] for f in range(F)]
        emit(a, carried)


def first_kernel(planes, group, halves, order, *refs):
    n = len(order)
    blocks, (lines, out, swapped, right_lines, fronts) = refs[:n], refs[n:]
    me = lax.rem(lax.axis_index("axial"), n)
    start = 0
    for target in (lines, right_lines):
        size = target.shape[0] // n
        for k, block in zip(order, blocks):
            target[pl.ds(pl.multiple_of((me ^ k) * size, 8), size), :] = block[start : start + size]
        start += size
    read = reader(lines, group, planes, ITEMS)
    read_right = reader(right_lines, group, planes, F)

    def emit(a, values):
        for f in range(F):
            at = (a * F + f) * group
            out[at : at + group, :] = values[f]
            swapped[at : at + halves, :] = values[f][halves:]
            swapped[at + halves : at + group, :] = values[f][:halves]

    last = n * planes
    vector = forward(read, lambda a: [read_right(a, f) for f in range(F)], last, group, fronts)
    backward(read, vector, last, fronts, emit)


def middle_kernel(
    planes, group, halves, part, lines, value, swapped, spectral, ready, mix, spread, prod
):
    read = reader(lines, group, planes, ITEMS)
    inst = spectral.shape[0]
    wide = halves * LANES
    mix[...] = jnp.zeros_like(mix)
    mix[0:inst, 0:inst] = spectral[...]
    lane = lax.broadcasted_iota(jnp.int32, (HP, wide), 1)
    instance = lax.broadcasted_iota(jnp.int32, (HP, wide), 0)
    shift = part.bit_length() - 1
    chosen = jnp.where(lax.shift_right_logical(lane, shift) == instance, 1.0, 0.0)
    over = lax.dot_general(
        mix[...], chosen, (((0,), (0,)), ((), ())), precision=HIGHEST, preferred_element_type=jnp.float32
    )
    over = lax.dot_general(
        chosen, over, (((0,), (0,)), ((), ())), precision=HIGHEST, preferred_element_type=jnp.float32
    )
    same = (lax.broadcasted_iota(jnp.int32, (wide, wide), 0) & (part - 1)) == (
        lax.broadcasted_iota(jnp.int32, (wide, wide), 1) & (part - 1)
    )
    spread[...] = jnp.where(same, over, 0.0)
    count = value.shape[0] // halves
    whole = jnp.concatenate(
        [value[pl.ds(half, count, stride=halves), :] for half in range(halves)], axis=1
    )
    mixed = jnp.dot(whole, spread[...], precision=HIGHEST, preferred_element_type=jnp.float32)
    for half in range(halves):
        prod[pl.ds(half, count, stride=halves), :] = mixed[:, half * LANES : (half + 1) * LANES]
    for a in range(value.shape[0] // (F * group)):
        side = read(a, SIDE)
        for f in range(F):
            at = (a * F + f) * group
            ready[at : at + group, :] = (
                read(a, SOURCE + f) + side * swapped[at : at + group, :] - prod[at : at + group, :]
            )


def collect_kernel(waited, *refs):
    *pieces, out = refs
    for i, piece in enumerate(pieces):
        out[i] = piece[...]


def forward_kernel(planes, group, halves, lines, ready, from_left, from_right, fronts, end):
    read = reader(lines, group, planes, ITEMS)
    last = lines.shape[0] // (group * planes * ITEMS) * planes
    first = lax.broadcasted_iota(jnp.int32, (group, LANES), 0) < halves

    def right(a):
        side = read(a, SIDE)
        result = []
        for f in range(F):
            at = (a * F + f) * group
            halo = jnp.where(first, from_left[at : at + group, :], from_right[at : at + group, :])
            result.append(ready[at : at + group, :] + side * halo)
        return result

    vector = forward(read, right, last, group, fronts)
    for f in range(F):
        end[f] = vector[f]


def second_kernel(
    planes, group, halves, part, azim, lines, fronts, end, face, crossed, partner, out
):
    read = reader(lines, group, planes, ITEMS)
    last = lines.shape[0] // (group * planes * ITEMS) * planes
    shift = part.bit_length() - 1
    rows = group // halves
    count = F * group
    mine, axial = lax.axis_index("azim"), lax.axis_index("axial")
    owners = last // planes
    me = lax.rem(axial, owners)
    chip, core = lax.shift_right_logical(me, 1), me & 1
    lane_at = lax.broadcasted_iota(jnp.int32, (count, LANES), 1)
    row_cell = lax.broadcasted_iota(jnp.int32, (F, rows, halves, LANES), 1).reshape(count, LANES)
    cells, accs = [], []
    for j in range(rows):
        own = jnp.broadcast_to(face[j : j + 1, :], (count, LANES))
        cell = jnp.take_along_axis(own, me * part + (lane_at & (part - 1)), axis=1)
        block = jnp.where(axial < owners, lax.shift_right_logical(cell, shift) - row_cell * owners, -1)
        cells.append((block, (lane_at & (LANES - part)) + (cell & (part - 1))))
        accs.append(jnp.zeros((count, LANES), jnp.float32))
    for side, buffers in enumerate((crossed, partner)):
        sender = core ^ side
        for at in range(buffers.shape[0]):
            k, i = at // azim, at % azim
            for q in range(2):
                owner = (chip ^ (2 * k + sender)) * 2 + (sender ^ q)
                block = lax.rem(mine - i + azim, azim) * (rows * owners) + owner
                values = buffers[at, q]
                for j in range(rows):
                    accs[j] = jnp.where(
                        cells[j][0] == block, jnp.take_along_axis(values, cells[j][1], axis=1), accs[j]
                    )
    picked = [
        [
            sum(accs[j][(f * rows + p) * halves : (f * rows + p + 1) * halves] for p in range(rows))
            for f in range(F)
        ]
        for j in range(rows)
    ]
    upper = read(last - 1, UPPER)
    vector = [
        end[f] - upper * jnp.concatenate([picked[j][f] for j in range(rows)], axis=0) for f in range(F)
    ]

    def emit(a, values):
        for f in range(F):
            at = (a * F + f) * group
            out[at : at + group, :] = values[f]

    backward(read, vector, last, fronts, emit)


def unpack_kernel(halves, part, value, out, turned, block):
    n, count, _ = value.shape
    planes, _, inst, rows, _ = out.shape
    per_row = LANES // part
    for d in range(n):
        part_rows = value[d].T
        for h8 in range(per_row):
            turned[h8, d * part : (d + 1) * part, :] = part_rows[h8 * part : (h8 + 1) * part]
    for h8 in range(per_row):
        block[h8] = turned[h8].T
        for a in range(planes):
            for f in range(F):
                for half in range(halves):
                    h = half * per_row + h8
                    at = (a * F + f) * rows * halves + half
                    if h < inst:
                        out[a, f, h] = block[h8, pl.ds(at, rows, stride=halves), :]


def shards(adjoint_source, adjoint_prev, diag_inverse, coupling, spectral, face_map):
    n, azim = lax.axis_size("axial") // 2, lax.axis_size("azim")
    planes, rows, _, inst, radial = adjoint_source.shape
    source = adjoint_source.transpose(0, 2, 3, 1, 4)
    prev = adjoint_prev.transpose(0, 2, 3, 1, 4)
    diag = diag_inverse.transpose(0, 2, 3, 4, 1, 5)
    coupling = coupling.transpose(0, 1, 3, 2, 4)
    part = radial // n
    halves = HP * part // LANES
    group = rows * halves
    axial = [list(range(n)), list(range(n, 2 * n))]
    both = ("axial", "azim")
    f32 = jnp.float32
    last = n * planes

    def around(up, down):
        forward = [(i, (i + 1) % azim) for i in range(azim)]
        backward = [((i + 1) % azim, i) for i in range(azim)]
        if azim == 2:
            got = lax.ppermute(up, "azim", forward)
            return got, got
        return lax.ppermute(up, "azim", forward), lax.ppermute(down, "azim", backward)

    size, count = planes * ITEMS, planes * F
    hbm, vmem = pl.BlockSpec(memory_space=pltpu.HBM), pl.BlockSpec(memory_space=pltpu.VMEM)

    def like(x, *lead):
        return jax.ShapeDtypeStruct(lead or x.shape, x.dtype)

    face = face_map.reshape(rows, radial)
    size, count = planes * ITEMS, planes * F
    block = jax.ShapeDtypeStruct((group * (size + count), LANES), f32)
    hbm, vmem = pl.BlockSpec(memory_space=pltpu.HBM), pl.BlockSpec(memory_space=pltpu.VMEM)
    left, right = around(prev, prev)
    inputs = (source, prev, diag, coupling, spectral, face)
    source, prev, diag, coupling, spectral, face, first = pl.pallas_call(
        fetch_kernel,
        in_specs=[hbm] * 6,
        out_shape=[jax.ShapeDtypeStruct(x.shape, x.dtype) for x in inputs]
        + [jax.ShapeDtypeStruct(prev.shape[1:], f32)],
        scratch_shapes=[pltpu.SemaphoreType.DMA((7,))],
        compiler_params=params(),
        name="fetch",
    )(*(pltpu.with_memory_space_constraint(x, pltpu.HBM) for x in inputs))
    facing = [
        lax.ppermute(
            first, both, [(n * azim + y, (n - 1) * azim + (y + k) % azim) for y in range(azim)]
        )
        for k in range(azim)
    ]
    *packed, base = pl.pallas_call(
        functools.partial(pack_kernel, n),
        out_shape=[jax.ShapeDtypeStruct((group * size, LANES), f32)] * n
        + [jax.ShapeDtypeStruct((rows * count, HP, LANES), f32)],
        scratch_shapes=[
            pltpu.VMEM((rows * size, HP, LANES), f32),
            pltpu.VMEM((n, halves, LANES, rows * size), f32),
            pltpu.VMEM((HP, HP), f32),
            pltpu.VMEM((HP, rows * count * LANES), f32),
        ],
        compiler_params=params(),
        name="pack",
    )(source, prev, diag, coupling, spectral)
    packed = pl.pallas_call(
        functools.partial(right_kernel, n, azim),
        out_shape=[block] * n,
        scratch_shapes=[
            pltpu.VMEM((rows * count, HP, LANES), f32),
            pltpu.VMEM((n, halves, LANES, rows * count), f32),
        ],
        compiler_params=params(),
        name="right_side",
    )(*facing, left, right, prev, coupling, base, face, *packed)
    order = sorted(range(n), key=lambda k: (k & 1, -bin(k & ~1).count("1"), k))
    blocks = [
        lax.ppermute(packed[k], "axial", [(i, i ^ k) for i in range(2 * n)]) if k else packed[k]
        for k in order
    ]
    shape = jax.ShapeDtypeStruct((last * F * group, LANES), f32)
    scratch = pltpu.VMEM((last, F, group, LANES), f32)
    lines, value, swapped = pl.pallas_call(
        functools.partial(first_kernel, planes, group, halves, order),
        out_shape=(jax.ShapeDtypeStruct((n * group * size, LANES), f32), shape, shape),
        scratch_shapes=[pltpu.VMEM((n * group * count, LANES), f32), scratch],
        compiler_params=params(),
        name="first_sweep",
    )(*blocks)
    from_left, from_right = around(swapped, swapped)
    piece = value[: F * group]
    core = [(i, i ^ 1) for i in range(2 * n)]
    chip = jnp.stack([piece, lax.ppermute(piece, "axial", core)])
    chips = n // 2
    crossed = []
    for k in range(chips // 2):
        for i in range(azim):
            there = [
                ((n + 2 * c + b) * azim + y, (2 * (c ^ (2 * k + b)) + b) * azim + (y + i) % azim)
                for c in range(chips)
                for b in range(2)
                for y in range(azim)
            ]
            crossed.append(lax.ppermute(chip, both, there + [(b, a) for a, b in there]))
    ready = pl.pallas_call(
        functools.partial(middle_kernel, planes, group, halves, part),
        out_shape=shape,
        scratch_shapes=[
            pltpu.VMEM((HP, HP), f32),
            pltpu.VMEM((halves * LANES, halves * LANES), f32),
            pltpu.VMEM((last * F * group, LANES), f32),
        ],
        compiler_params=params(),
        name="spectral_term",
    )(lines, value, swapped, spectral)
    crossed = pl.pallas_call(
        collect_kernel,
        in_specs=[pl.BlockSpec(memory_space=pl.ANY)] + [vmem] * len(crossed),
        out_shape=jax.ShapeDtypeStruct((len(crossed),) + chip.shape, f32),
        compiler_params=params(),
        name="collect",
    )(ready, *crossed)
    partner = lax.ppermute(crossed, "axial", core)
    fronts, end = pl.pallas_call(
        functools.partial(forward_kernel, planes, group, halves),
        out_shape=(
            jax.ShapeDtypeStruct((last, F, group, LANES), f32),
            jax.ShapeDtypeStruct((F, group, LANES), f32),
        ),
        compiler_params=params(),
        name="second_forward",
    )(lines, ready, from_left, from_right)
    value = pl.pallas_call(
        functools.partial(second_kernel, planes, group, halves, part, azim),
        out_shape=shape,
        compiler_params=params(),
        name="second_backward",
    )(lines, fronts, end, face, crossed, partner)
    value = lax.all_to_all(
        value.reshape(n, planes * F * group, LANES), "axial", 0, 0, axis_index_groups=axial, tiled=True
    )
    out = pl.pallas_call(
        functools.partial(unpack_kernel, halves, part),
        out_shape=jax.ShapeDtypeStruct(source.shape, f32),
        scratch_shapes=[
            pltpu.VMEM((LANES // part, LANES, planes * F * group), f32),
            pltpu.VMEM((LANES // part, planes * F * group, LANES), f32),
        ],
        compiler_params=params(),
        name="unpack",
    )(value)
    return out.transpose(0, 3, 1, 2, 4)


def solution(mesh):
    placed = (
        P("axial", "azim", None, None, None),
        P("axial", "azim", None, None, None),
        P("axial", "azim", None, None, None, None),
        P(None, "axial", "azim", None, None),
        P(),
        P("azim"),
    )
    return jax.shard_map(
        shards,
        mesh=mesh,
        in_specs=placed,
        out_specs=P("axial", "azim", None, None, None),
        check_vma=False,
    )
```
